32 devices in a mesh: dp: 4 (over y, core), fsdp: 8 (over z, x).
Axes of the slice: x: 2, y: 2, z: 4, core: 2. Of those that a mesh axis runs over, the one named last changes fastest.
Arguments:
- cells: bfloat16 [32768, 1024], P(('dp', 'fsdp')), may hold values from -6 to 6
- segment_ids: int32 [32, 1024], P(('dp', 'fsdp')), may hold values from 0 to 7, never falling along the last dimension, each value on 1 to 256 neighbouring positions
- valid: int32 [32, 1024], P(('dp', 'fsdp')), may hold values 0 or 1
- norm1_gain: bfloat16 [1024], P(('dp', 'fsdp')), may hold values from 0.5 to 1.5
- norm1_bias: bfloat16 [1024], P(('dp', 'fsdp')), may hold values from -3 to 3
- qkv_weight: bfloat16 [1024, 3072], P(('dp', 'fsdp')), may hold values from -0.1875 to 0.1875
- qv_bias: bfloat16 [2048], P(('dp', 'fsdp')), may hold values from -1 to 1
- out_weight: bfloat16 [1024, 1024], P(('dp', 'fsdp')), may hold values from -0.75 to 0.75
- out_bias: bfloat16 [1024], P(('dp', 'fsdp')), may hold values from -3 to 3
- norm2_gain: bfloat16 [1024], P(('dp', 'fsdp')), may hold values from 0.5 to 1.5
- norm2_bias: bfloat16 [1024], P(('dp', 'fsdp')), may hold values from -3 to 3
- up_weight: bfloat16 [1024, 4096], P(('dp', 'fsdp')), may hold values from -0.1875 to 0.1875
- up_bias: bfloat16 [4096], P(('dp', 'fsdp')), may hold values from -3 to 3
- down_weight: bfloat16 [4096, 1024], P(('dp', 'fsdp')), may hold values from -0.125 to 0.125
- down_bias: bfloat16 [1024], P(('dp', 'fsdp')), may hold values from -3 to 3
- out_grad: bfloat16 [32768, 1024], P(('dp', 'fsdp')), may hold values from -6 to 6
Outputs:
- out_cells: bfloat16 [32768, 1024], P(('dp', 'fsdp'))
- cells_grad: bfloat16 [32768, 1024], P(('dp', 'fsdp'))
- norm1_gain_grad: float32 [1024], P(('dp', 'fsdp'))
- norm1_bias_grad: float32 [1024], P(('dp', 'fsdp'))
- qkv_weight_grad: float32 [1024, 3072], P(('dp', 'fsdp'))
- qv_bias_grad: float32 [2048], P(('dp', 'fsdp'))
- out_weight_grad: float32 [1024, 1024], P(('dp', 'fsdp'))
- out_bias_grad: float32 [1024], P(('dp', 'fsdp'))
- norm2_gain_grad: float32 [1024], P(('dp', 'fsdp'))
- norm2_bias_grad: float32 [1024], P(('dp', 'fsdp'))
- up_weight_grad: float32 [1024, 4096], P(('dp', 'fsdp'))
- up_bias_grad: float32 [4096], P(('dp', 'fsdp'))
- down_weight_grad: float32 [4096, 1024], P(('dp', 'fsdp'))
- down_bias_grad: float32 [1024], P(('dp', 'fsdp'))
The draws below stay inside these ranges and needn't reach their ends.
Inputs may be any that keep to these rules, and one draw needn't show every extreme that they name: `segment_ids`: along each row the slide numbers never fall; each slide covers 1 to 256 consecutive cells. `valid`: 1 marks a real cell, 0 padding, anywhere in a row.
All inputs are finite; a program needn't handle non-finite values. No bound on the sum of `valid` on one device may be relied on, other than what follows from the above.
Results may differ from the reference program's by a relative error of at most 0.013.
Values may be sent and summed in bfloat16 or wider, within the bound.
No kernel may reach another device: no remote copies, remote signals or barrier semaphores. Data moves between devices by JAX's collectives and lax.ppermute only.
A program may use at most 256 MiB of HBM per device.

```python
import math
import jax
import jax.numpy as jnp
import numpy as np
from jax import lax

D = 1024
HEADS = 16
HEAD = 64
FF = 4096
TOK_DEV = 1024
SLIDES = 8
SEQS = 32
TOKENS = 32768


def set_ends(drawn, key, low, high):
    longest = drawn.shape.index(max(drawn.shape))
    spots = []
    for shift in (0, 1):
        where = [jax.random.randint(jax.random.fold_in(key, axis), (), 0, length) for axis, length in enumerate(drawn.shape)]
        where[longest] = (where[longest] + shift) % drawn.shape[longest]
        spots.append(tuple(where))
    return drawn.at[spots[0]].set(low).at[spots[1]].set(high)


def levels(own_key, extent, pieces, least, largest):
    def one(dim, blocks):
        heights = jax.random.uniform(jax.random.fold_in(jax.random.fold_in(own_key, 6), dim), (blocks,), jnp.float32, least / len(pieces), largest / len(pieces))
        return jnp.repeat(jnp.exp(heights), extent[dim] // blocks).reshape((-1,) + (1,) * (len(extent) - dim - 1))

    factor_of = one(*pieces[0])
    for cut in pieces[1:]:
        factor_of = factor_of * one(*cut)
    return factor_of


def length_profile(count, total, reach, lean):
    weights = [(1 << 20) // math.isqrt(standing ** lean) + 1 for standing in range(2, count + 1)]
    surplus, holding = total - reach - (count - 1), [1] * (count - 1)
    while surplus > 0:
        movable = [i for i in range(count - 1) if holding[i] < reach]
        pool, remaining = sum([weights[i] for i in movable]), surplus
        for i in movable:
            addition = min(reach - holding[i], max(1, remaining * weights[i] // pool), surplus)
            holding[i] = holding[i] + addition
            surplus = surplus - addition
    return np.array([reach] + holding)


def ragged(rng, count, total, reach, skew):
    if count == 2:
        one = jax.random.randint(rng, (), max(1, total - reach), min(reach, total - 1) + 1)
        return jnp.stack([one, total - one])
    tallies = jnp.asarray(length_profile(count, total, reach, skew), jnp.int32)
    twos = (count - 1) // 2
    giver, taker = tallies[1:1 + 2 * twos:2], tallies[2:2 + 2 * twos:2]
    margin = jnp.minimum(giver - 1, reach - taker)
    passed = jax.random.randint(jax.random.fold_in(rng, 1), (twos,), 0, 1 << 20) % (margin + 1)
    tallies = tallies.at[1:1 + 2 * twos:2].set(giver - passed).at[2:2 + 2 * twos:2].set(taker + passed)
    return tallies[jax.random.permutation(jax.random.fold_in(rng, 2), count)]


def gaussian(stream_key, extent, scale, bound, cuts=(), held_as=jnp.bfloat16):
    array = scale * jax.random.normal(stream_key, extent, jnp.float32)
    if cuts:
        array = array * levels(stream_key, extent, cuts, -0.22, 0.18)
    return jnp.clip(array, -bound, bound).astype(held_as)


def setup_inputs(seed: int = 0) -> dict:
    key_of = jax.random.split(jax.random.key(seed), 17)
    cells = gaussian(key_of[0], (TOKENS, D), 1.0, 6.0, ((0, 32),))
    segment_ids = jax.vmap(lambda own: jnp.searchsorted(jnp.cumsum(ragged(own, SLIDES, TOK_DEV, TOK_DEV // 4, 1)), jnp.arange(TOK_DEV), side="right"))(jax.random.split(key_of[1], SEQS)).reshape((SEQS, TOK_DEV)).astype(jnp.int32)
    valid = set_ends((jax.random.randint(key_of[2], (SEQS, TOK_DEV), 0, 8) < 7).astype(jnp.int32), jax.random.fold_in(key_of[2], 1), 0, 1)
    norm1_gain = jnp.clip(1.0 + 0.1 * jax.random.normal(key_of[3], (D,), jnp.float32), 0.5, 1.5).astype(jnp.bfloat16)
    norm1_bias = gaussian(key_of[4], (D,), 0.3, 3.0, ((0, 32),))
    qkv_weight = gaussian(key_of[5], (D, 3 * D), D ** -0.5, 0.1875, ((0, 32),))
    qv_bias = gaussian(key_of[6], (2 * D,), 0.1, 1.0, ((0, 32),))
    out_weight = gaussian(key_of[7], (D, D), (D // 16) ** -0.5, 0.75, ((0, 32),))
    out_bias = gaussian(key_of[8], (D,), 0.3, 3.0, ((0, 32),))
    norm2_gain = jnp.clip(1.0 + 0.1 * jax.random.normal(key_of[9], (D,), jnp.float32), 0.5, 1.5).astype(jnp.bfloat16)
    norm2_bias = gaussian(key_of[10], (D,), 0.3, 3.0, ((0, 32),))
    up_weight = gaussian(key_of[11], (D, FF), D ** -0.5, 0.1875, ((0, 32),))
    up_bias = gaussian(key_of[12], (FF,), 0.5, 3.0, ((0, 32),))
    down_weight = gaussian(key_of[13], (FF, D), (FF // 2) ** -0.5, 0.125, ((0, 32),))
    down_bias = gaussian(key_of[14], (D,), 0.3, 3.0, ((0, 32),))
    out_grad = gaussian(key_of[15], (TOKENS, D), 1.0, 6.0, ((0, 32),))
    return dict(cells=cells, segment_ids=segment_ids, valid=valid, norm1_gain=norm1_gain, norm1_bias=norm1_bias, qkv_weight=qkv_weight, qv_bias=qv_bias, out_weight=out_weight, out_bias=out_bias, norm2_gain=norm2_gain, norm2_bias=norm2_bias, up_weight=up_weight, up_bias=up_bias, down_weight=down_weight, down_bias=down_bias, out_grad=out_grad)


@jax.custom_vjp
def low(v):
    return lax.optimization_barrier(v.astype(jnp.bfloat16)).astype(jnp.float32)

@jax.custom_vjp
def low_back(v):
    return v

def low_keep(v):
    return (low(v), None)

def low_pass(kept, grad):
    return (grad,)

def back_keep(v):
    return (v, None)

def back_low(kept, grad):
    return (low(grad),)
low.defvjp(low_keep, low_pass)
low_back.defvjp(back_keep, back_low)
EPSILON = 1e-05
HIGHEST = lax.Precision.HIGHEST

def norm_rows(cell_rows, gain_vec, shift_vec):
    row_mean = lax.optimization_barrier(jnp.mean(cell_rows, axis=-1, keepdims=True))
    centred = cell_rows - row_mean
    row_var = lax.optimization_barrier(jnp.mean(centred * centred, axis=-1, keepdims=True))
    return centred * lax.rsqrt(row_var + EPSILON) * gain_vec + shift_vec

def layer(cell_rows, slide_ids, live_keys, params):
    gain_one, shift_one, qkv_weight, qv_bias, out_weight, out_bias, gain_two, shift_two, up_weight, up_bias, down_weight, down_bias = params
    num_rows, model_width = cell_rows.shape
    score_scale = 1.0 / math.sqrt(HEAD)
    normed = low(norm_rows(cell_rows, gain_one, shift_one))
    key_zeros = jnp.zeros((model_width,), jnp.float32)
    bias_full = jnp.concatenate([qv_bias[:model_width], key_zeros, qv_bias[model_width:]])
    qkv_all = jnp.dot(normed, qkv_weight, precision=HIGHEST) + bias_full
    query_heads = low(low_back(qkv_all[:, :model_width])).reshape(num_rows, HEADS, HEAD)
    key_heads = low(low_back(qkv_all[:, model_width:2 * model_width])).reshape(num_rows, HEADS, HEAD)
    value_heads = low(low_back(qkv_all[:, 2 * model_width:])).reshape(num_rows, HEADS, HEAD)
    positions = jnp.arange(num_rows)
    allowed = (slide_ids[:, None] == slide_ids[None, :]) & ((live_keys[None, :] == 1) | (positions[:, None] == positions[None, :]))
    scores = jnp.einsum('qhe,khe->hqk', query_heads, key_heads, precision=HIGHEST) * score_scale
    scores = low_back(jnp.where(allowed[None], scores, -1e+30))
    top_score = lax.optimization_barrier(jnp.max(scores, axis=-1, keepdims=True))
    expd = jnp.exp(scores - top_score)
    probs = low(expd / lax.optimization_barrier(jnp.sum(expd, axis=-1, keepdims=True)))
    mixed = jnp.einsum('hqk,khe->qhe', probs, value_heads, precision=HIGHEST).reshape(num_rows, model_width)
    mixed = low(low_back(mixed))
    branch = low_back(jnp.dot(mixed, out_weight, precision=HIGHEST) + out_bias)
    inner = cell_rows + branch
    normed_two = low(norm_rows(inner, gain_two, shift_two))
    up_proj = low_back(jnp.dot(normed_two, up_weight, precision=HIGHEST) + up_bias)
    hidden = low(jax.nn.gelu(up_proj, approximate=False))
    ffn_out = low_back(jnp.dot(hidden, down_weight, precision=HIGHEST) + down_bias)
    return inner + ffn_out

def reference(cells, segment_ids, valid, norm1_gain, norm1_bias, qkv_weight, qv_bias, out_weight, out_bias, norm2_gain, norm2_bias, up_weight, up_bias, down_weight, down_bias, out_grad):
    params = tuple((param.astype(jnp.float32) for param in (norm1_gain, norm1_bias, qkv_weight, qv_bias, out_weight, out_bias, norm2_gain, norm2_bias, up_weight, up_bias, down_weight, down_bias)))
    rows_all = cells.astype(jnp.float32).reshape(SEQS, TOK_DEV, D)
    cot_all = out_grad.astype(jnp.float32).reshape(SEQS, TOK_DEV, D)

    def per_sequence(grad_total, seq_item):
        cell_rows, slide_ids, live_keys, cot_rows = seq_item

        def apply_layer(rows_in, params_in):
            return layer(rows_in, slide_ids, live_keys, params_in)
        layer_out, pull_back = jax.vjp(apply_layer, cell_rows, params)
        d_rows, d_params = pull_back(cot_rows)
        grad_total = jax.tree.map(lambda left, right: left + right, grad_total, d_params)
        return (grad_total, (layer_out.astype(jnp.bfloat16), d_rows.astype(jnp.bfloat16)))
    start_total = tuple((jnp.zeros(param.shape, jnp.float32) for param in params))
    grad_total, (outs_all, dcells_all) = lax.scan(per_sequence, start_total, (rows_all, segment_ids, valid, cot_all))
    return (outs_all.reshape(TOKENS, D), dcells_all.reshape(TOKENS, D), grad_total[0], grad_total[1], grad_total[2], grad_total[3], grad_total[4], grad_total[5], grad_total[6], grad_total[7], grad_total[8], grad_total[9], grad_total[10], grad_total[11])
```

```python
from functools import partial
import math

import jax
import jax.numpy as jnp
from jax import lax
from jax.experimental import pallas as pl
from jax.experimental.pallas import tpu as pltpu
from jax.sharding import Mesh, PartitionSpec as P

HEADS = 16
HEAD = 64


EPSILON = 1e-05


def norm_rows(cell_rows, gain_vec, shift_vec):
    row_mean = jnp.mean(cell_rows, axis=-1, keepdims=True)
    centred = cell_rows - row_mean
    row_var = jnp.mean(centred * centred, axis=-1, keepdims=True)
    return centred * lax.rsqrt(row_var + EPSILON) * gain_vec + shift_vec


def norm_pull(cell_rows, gain_vec):
    zero_shift = jnp.zeros_like(gain_vec)
    normed_rows, pull_back = jax.vjp(norm_rows, cell_rows, gain_vec, zero_shift)
    return pull_back


def gelu_exact(values_in):
    return jax.nn.gelu(values_in, approximate=False)


def times_left(left_mat, right_mat):
    return lax.dot_general(
        left_mat, right_mat, (((0,), (0,)), ((), ())), preferred_element_type=jnp.float32
    )


def times_right(left_mat, right_mat):
    return lax.dot_general(
        left_mat, right_mat, (((1,), (1,)), ((), ())), preferred_element_type=jnp.float32
    )


def group_heads(tensor, num_groups):
    return tensor.reshape(tensor.shape[0], num_groups, -1).transpose(1, 0, 2)


def ungroup(tensor):
    return tensor.transpose(1, 0, 2).reshape(tensor.shape[1], -1)


def allowed_rows(slide_ids, live_keys, row_start, block_rows):
    num_rows = slide_ids.shape[0]
    row_places = row_start + jnp.arange(block_rows)
    col_places = jnp.arange(num_rows)
    same_slide = slide_ids[row_start : row_start + block_rows][:, None] == slide_ids[None, :]
    open_key = (live_keys[None, :] == 1) | (row_places[:, None] == col_places[None, :])
    return same_slide & open_key


def attend_forward(mask_blocks, block_rows, score_scale, group_item):
    query, key_rows, value_rows = group_item
    num_rows = query.shape[0]
    heads_here = query.shape[1] // HEAD
    query_heads = query.reshape(num_rows, heads_here, HEAD)
    key_heads = key_rows.reshape(num_rows, heads_here, HEAD)
    value_heads = value_rows.reshape(num_rows, heads_here, HEAD)
    out_parts = []
    lse_parts = []
    for block_id, row_start in enumerate(range(0, num_rows, block_rows)):
        scores = (
            jnp.einsum(
                "qhe,khe->hqk",
                query_heads[row_start : row_start + block_rows],
                key_heads,
                preferred_element_type=jnp.float32,
            )
            * score_scale
        )
        scores = jnp.where(mask_blocks[block_id][None], scores, -1e30)
        top_score = jnp.max(scores, axis=-1, keepdims=True)
        expd = jnp.exp(scores - top_score)
        row_total = jnp.sum(expd, axis=-1, keepdims=True)
        probs = (expd / row_total).astype(jnp.bfloat16)
        mixed = jnp.einsum("hqk,khe->qhe", probs, value_heads, preferred_element_type=jnp.float32)
        out_parts.append(mixed.astype(jnp.bfloat16).reshape(block_rows, -1))
        lse_parts.append((top_score + jnp.log(row_total))[..., 0])
    return (jnp.concatenate(out_parts, 0), jnp.concatenate(lse_parts, 1))


def attend_backward(mask_blocks, block_rows, score_scale, group_item):
    query, key_rows, value_rows, grad_rows, log_sums = group_item
    num_rows = query.shape[0]
    heads_here = query.shape[1] // HEAD
    query_heads = query.reshape(num_rows, heads_here, HEAD)
    key_heads = key_rows.reshape(num_rows, heads_here, HEAD)
    value_heads = value_rows.reshape(num_rows, heads_here, HEAD)
    grad_heads = grad_rows.reshape(num_rows, heads_here, HEAD)
    d_key_sum = jnp.zeros((num_rows, heads_here, HEAD), jnp.float32)
    d_value_sum = jnp.zeros((num_rows, heads_here, HEAD), jnp.float32)
    d_query_parts = []
    for block_id, row_start in enumerate(range(0, num_rows, block_rows)):
        query_block = query_heads[row_start : row_start + block_rows]
        grad_block = grad_heads[row_start : row_start + block_rows]
        scores = (
            jnp.einsum("qhe,khe->hqk", query_block, key_heads, preferred_element_type=jnp.float32)
            * score_scale
        )
        scores = jnp.where(mask_blocks[block_id][None], scores, -1e30)
        probs = jnp.exp(scores - log_sums[:, row_start : row_start + block_rows, None])
        d_value_sum = d_value_sum + jnp.einsum(
            "hqk,qhe->khe",
            probs.astype(jnp.bfloat16),
            grad_block,
            preferred_element_type=jnp.float32,
        )
        d_probs = jnp.einsum(
            "qhe,khe->hqk", grad_block, value_heads, preferred_element_type=jnp.float32
        )
        d_scores = (probs * (d_probs - jnp.sum(probs * d_probs, axis=-1, keepdims=True))).astype(
            jnp.bfloat16
        )
        d_query_block = (
            jnp.einsum("hqk,khe->qhe", d_scores, key_heads, preferred_element_type=jnp.float32)
            * score_scale
        )
        d_query_parts.append(d_query_block.astype(jnp.bfloat16).reshape(block_rows, -1))
        d_key_sum = d_key_sum + jnp.einsum(
            "hqk,qhe->khe", d_scores, query_block, preferred_element_type=jnp.float32
        )
    d_keys = (d_key_sum * score_scale).astype(jnp.bfloat16).reshape(num_rows, -1)
    d_values = d_value_sum.astype(jnp.bfloat16).reshape(num_rows, -1)
    return (jnp.concatenate(d_query_parts, 0), d_keys, d_values)


AXES = ("y", "core", "z", "x")


def ring(num):
    return [(place, (place + 1) % num) for place in range(num)]


class Grid:
    def __init__(self, sizes):
        self.sizes = dict(zip(AXES, sizes))
        self.total = math.prod(sizes)

    def coords(self):
        return {name: lax.axis_index(name) for name in AXES}

    def block(self, coords):
        place = 0
        for name in AXES:
            place = place * self.sizes[name] + coords[name]
        return place


def gather_pieces(grid, own, order):
    held = [own[None]]
    for name in order:
        held = [jnp.concatenate(held, 0) if len(held) > 1 else held[0]]
        for _ in range(grid.sizes[name] - 1):
            held.append(lax.ppermute(held[-1], name, ring(grid.sizes[name])))
    return held


def block_places(grid, coords, order, piece):
    sizes = [grid.sizes[name] for name in order]
    inner = math.prod(sizes[:-1])
    places = []
    for slot in range(inner):
        here = dict(coords)
        left = slot
        for name, size in zip(order[:-1], sizes[:-1]):
            here[name] = lax.rem(coords[name] - left % size + size, size)
            left //= size
        here[order[-1]] = lax.rem(coords[order[-1]] - piece + sizes[-1], sizes[-1])
        places.append(grid.block(here))
    return places


def assemble_kernel(plan, num_in, *refs):
    places, ins, outs, sem = refs[0], refs[1 : 1 + num_in], refs[1 + num_in : -1], refs[-1]
    copies = []
    for number, (block_id, cuts) in enumerate(plan):
        source, slot = block_id
        rows = ins[source].shape[1]
        for first, width, target, column in cuts:
            start = pl.multiple_of(places[number] * rows, rows)
            copies.append(
                pltpu.make_async_copy(
                    ins[source].at[slot, :, pl.ds(first, width)],
                    outs[target].at[pl.ds(start, rows), pl.ds(column, width)],
                    sem,
                )
            )
    for copy in copies:
        copy.start()
    for copy in copies:
        copy.wait()


def assemble(grid, coords, gathered, widths):
    rows = gathered[0][0][0].shape[1]
    arrays, plan, places = [], [], []
    for pieces, order, cuts in gathered:
        for number, piece in enumerate(pieces):
            for slot, place in enumerate(block_places(grid, coords, order, number)):
                plan.append(((len(arrays), slot), cuts))
                places.append(place)
            arrays.append(piece)
    all_rows = rows * grid.total
    if rows % 16:
        results = []
        for target, width in enumerate(widths):
            columns = []
            for pieces, order, cuts in gathered:
                for first, size, aim, column in cuts:
                    if aim == target:
                        spots = jnp.stack(
                            sum(
                                [
                                    block_places(grid, coords, order, number)
                                    for number in range(len(pieces))
                                ],
                                [],
                            )
                        )
                        stacked = jnp.concatenate(pieces, 0)[:, :, first : first + size]
                        placed = jnp.zeros_like(stacked).at[spots].set(stacked)
                        columns.append((column, placed.reshape(all_rows, size)))
            columns.sort(key=lambda item: item[0])
            results.append(jnp.concatenate([item[1] for item in columns], 1))
        return results
    return pl.pallas_call(
        partial(assemble_kernel, plan, len(arrays)),
        out_shape=[jax.ShapeDtypeStruct((all_rows, width), arrays[0].dtype) for width in widths],
        in_specs=[pl.BlockSpec(memory_space=pltpu.SMEM)]
        + [pl.BlockSpec(memory_space=pl.ANY)] * len(arrays),
        out_specs=[pl.BlockSpec(memory_space=pl.ANY)] * len(widths),
        scratch_shapes=[pltpu.SemaphoreType.DMA],
        cost_estimate=pl.CostEstimate(
            flops=0,
            bytes_accessed=4 * all_rows * sum(widths),
            transcendentals=0,
        ),
    )(jnp.stack(places).astype(jnp.int32), *arrays)


def scatter_stages(grid, coords, terms, axes, order, wire):
    axes = list(axes)
    for name in order:
        dim = axes.index(name)
        size = grid.sizes[name]
        arrived = None
        for step in range(size - 1):
            block = lax.rem(coords[name] + (2 * size - 1 - step), size)
            sent = sum(
                lax.dynamic_index_in_dim(term, block, dim, keepdims=False).astype(jnp.float32)
                for term in terms
            )
            if arrived is not None:
                sent = sent + arrived.astype(jnp.float32)
            arrived = lax.ppermute(sent.astype(wire), name, ring(size))
        terms = [
            lax.dynamic_index_in_dim(term, coords[name], dim, keepdims=False) for term in terms
        ] + [arrived]
        axes.remove(name)
    return sum(term.astype(jnp.float32) for term in terms)


def weight_grad(grid, coords, rows_in, cots):
    sizes = [grid.sizes[name] for name in AXES]
    rows = rows_in.shape[0]
    split = rows_in.reshape(rows, sizes[0], sizes[1], -1)

    def part(core):
        chosen = lax.dynamic_index_in_dim(split, core, 2, keepdims=False)
        product = times_left(chosen.reshape(rows, -1), cots).astype(jnp.bfloat16)
        return product.reshape(sizes[0], sizes[2], sizes[3], -1, cots.shape[1])

    sent = part(1 - coords["core"])
    arrived = lax.ppermute(sent, "core", ring(2))
    return [part(coords["core"]), arrived]


def local(
    grid,
    cells,
    segment_ids,
    valid,
    norm1_gain,
    norm1_bias,
    qkv_weight,
    qv_bias,
    out_weight,
    out_bias,
    norm2_gain,
    norm2_bias,
    up_weight,
    up_bias,
    down_weight,
    down_bias,
    out_grad,
):
    num_rows, model_width = cells.shape
    block_rows = min(512, num_rows)
    score_scale = 1.0 / math.sqrt(HEAD)
    per_group = min(4, HEADS)
    num_groups = HEADS // per_group
    slide_ids = segment_ids[0]
    live_keys = valid[0]
    mask_blocks = [
        allowed_rows(slide_ids, live_keys, row_start, block_rows)
        for row_start in range(0, num_rows, block_rows)
    ]
    coords = grid.coords()
    own_rows = qkv_weight.shape[0]
    vectors = (
        norm1_gain,
        norm1_bias,
        qv_bias,
        out_bias,
        norm2_gain,
        norm2_bias,
        up_bias,
        down_bias,
    )
    packed = jnp.concatenate(vectors)
    packed_size = packed.shape[0]
    packed = jnp.pad(packed, (0, own_rows * 128 - packed_size)).reshape(own_rows, 128)
    w_up = lax.all_gather(up_weight, AXES, axis=0, tiled=True)
    order_a = ("x", "z", "y", "core")
    order_b = ("y", "z", "x", "core")
    first_half = gather_pieces(grid, qkv_weight[:, : 2 * model_width], order_a)
    second_half = gather_pieces(
        grid,
        jnp.concatenate([qkv_weight[:, 2 * model_width :], out_weight, packed], 1),
        order_b,
    )
    w_qkv, w_out, all_packed = assemble(
        grid,
        coords,
        [
            (first_half, order_a, [(0, 2 * model_width, 0, 0)]),
            (
                second_half,
                order_b,
                [
                    (0, model_width, 0, 2 * model_width),
                    (model_width, model_width, 1, 0),
                    (2 * model_width, 128, 2, 0),
                ],
            ),
        ],
        [3 * model_width, model_width, 128],
    )
    down_own, _ = lax.optimization_barrier((down_weight, second_half[-1]))
    down_pieces = gather_pieces(grid, down_own, order_a)
    (w_down,) = assemble(
        grid, coords, [(down_pieces, order_a, [(0, model_width, 0, 0)])], [model_width]
    )
    all_packed = all_packed.reshape(grid.total, -1)[:, :packed_size]
    spread, first = [], 0
    for vector in vectors:
        size = vector.shape[0]
        spread.append(all_packed[:, first : first + size].reshape(-1))
        first += size
    gain_one, shift_one, b_qv, b_out, gain_two, shift_two, b_up, b_down = spread
    cell_rows = cells.astype(jnp.float32)
    normed = norm_rows(
        cell_rows, gain_one.astype(jnp.float32), shift_one.astype(jnp.float32)
    ).astype(jnp.bfloat16)
    qkv_all = jnp.dot(normed, w_qkv, preferred_element_type=jnp.float32)
    bias_float = b_qv.astype(jnp.float32)
    query = (qkv_all[:, :model_width] + bias_float[:model_width]).astype(jnp.bfloat16)
    key_rows = qkv_all[:, model_width : 2 * model_width].astype(jnp.bfloat16)
    value_rows = (qkv_all[:, 2 * model_width :] + bias_float[model_width:]).astype(jnp.bfloat16)
    query_groups = group_heads(query, num_groups)
    key_groups = group_heads(key_rows, num_groups)
    value_groups = group_heads(value_rows, num_groups)
    mixed_groups, lse_groups = lax.map(
        partial(attend_forward, mask_blocks, block_rows, score_scale),
        (query_groups, key_groups, value_groups),
    )
    mixed = ungroup(mixed_groups)
    inner = (
        cell_rows
        + jnp.dot(mixed, w_out, preferred_element_type=jnp.float32)
        + b_out.astype(jnp.float32)
    )
    normed_two = norm_rows(
        inner, gain_two.astype(jnp.float32), shift_two.astype(jnp.float32)
    ).astype(jnp.bfloat16)
    up_proj = jnp.dot(normed_two, w_up, preferred_element_type=jnp.float32) + b_up.astype(
        jnp.float32
    )
    hidden, gelu_back = jax.vjp(gelu_exact, up_proj)
    hidden_low = hidden.astype(jnp.bfloat16)
    layer_out = (
        inner
        + jnp.dot(hidden_low, w_down, preferred_element_type=jnp.float32)
        + b_down.astype(jnp.float32)
    )
    out_cells = layer_out.astype(jnp.bfloat16)
    cot_rows = out_grad.astype(jnp.float32)
    d_down = weight_grad(grid, coords, hidden_low, out_grad)
    d_down_bias = jnp.sum(cot_rows, axis=0)
    d_hidden = times_right(out_grad, w_down)
    (d_up_full,) = gelu_back(d_hidden)
    d_up_low = d_up_full.astype(jnp.bfloat16)
    d_up_weight = weight_grad(grid, coords, normed_two, d_up_low)
    d_up_bias = jnp.sum(d_up_low.astype(jnp.float32), axis=0)
    d_normed_two = times_right(d_up_low, w_up)
    pull_two = norm_pull(inner, gain_two.astype(jnp.float32))
    d_inner_part, d_gain_two, d_shift_two = pull_two(d_normed_two)
    d_inner = cot_rows + d_inner_part
    d_inner_low = d_inner.astype(jnp.bfloat16)
    d_out_weight = weight_grad(grid, coords, mixed, d_inner_low)
    d_out_bias = jnp.sum(d_inner_low.astype(jnp.float32), axis=0)
    d_mixed = times_right(d_inner_low, w_out).astype(jnp.bfloat16)
    d_query_g, d_key_g, d_value_g = lax.map(
        partial(attend_backward, mask_blocks, block_rows, score_scale),
        (query_groups, key_groups, value_groups, group_heads(d_mixed, num_groups), lse_groups),
    )
    d_query = ungroup(d_query_g)
    d_value = ungroup(d_value_g)
    d_qkv = jnp.concatenate([d_query, ungroup(d_key_g), d_value], axis=1)
    half_width = 3 * model_width // 2
    d_qkv_first = weight_grad(grid, coords, normed, d_qkv[:, :half_width])
    d_qkv_second = weight_grad(grid, coords, normed, d_qkv[:, half_width:])
    d_qv_bias = jnp.concatenate(
        [jnp.sum(d_query.astype(jnp.float32), axis=0), jnp.sum(d_value.astype(jnp.float32), axis=0)]
    )
    d_normed = times_right(d_qkv, w_qkv)
    pull_one = norm_pull(cell_rows, gain_one.astype(jnp.float32))
    d_rows_part, d_gain_one, d_shift_one = pull_one(d_normed)
    cells_grad = (d_inner + d_rows_part).astype(jnp.bfloat16)
    left_axes = ("y", "z", "x")

    def total(terms, order):
        return scatter_stages(grid, coords, terms, left_axes, order, jnp.bfloat16)

    down_total = total(d_down, ("x", "z", "y"))
    up_total = total(d_up_weight, ("y", "z", "x"))
    out_total = total(d_out_weight, ("x", "z", "y"))
    qkv_total = jnp.concatenate(
        [total(d_qkv_first, ("x", "z", "y")), total(d_qkv_second, ("y", "z", "x"))], 1
    )
    vector_grads = (
        d_gain_one,
        d_shift_one,
        d_qv_bias,
        d_out_bias,
        d_gain_two,
        d_shift_two,
        d_up_bias,
        d_down_bias,
    )
    sizes = [grid.sizes[name] for name in AXES]
    stacked = jnp.concatenate([grad.reshape(*sizes, -1) for grad in vector_grads], -1)
    summed = scatter_stages(
        grid, coords, [stacked], AXES, ("core", "x", "z", "y"), jnp.float32
    )
    parts, first = [], 0
    for vector in vectors:
        parts.append(summed[first : first + vector.shape[0]])
        first += vector.shape[0]
    return (
        out_cells,
        cells_grad,
        parts[0],
        parts[1],
        qkv_total,
        parts[2],
        out_total,
        parts[3],
        parts[4],
        parts[5],
        up_total,
        parts[6],
        down_total,
        parts[7],
    )


def solution(mesh):
    outer, inner_size = mesh.devices.shape
    sizes = (outer // 2, 2, inner_size // 2, 2)
    fine = Mesh(mesh.devices.reshape(sizes), AXES)
    rows, vector = P(AXES, None), P(AXES)
    return jax.shard_map(
        partial(local, Grid(sizes)),
        mesh=fine,
        in_specs=(
            rows,
            rows,
            rows,
            vector,
            vector,
            rows,
            vector,
            rows,
            vector,
            vector,
            vector,
            rows,
            vector,
            rows,
            vector,
            rows,
        ),
        out_specs=(
            rows,
            rows,
            vector,
            vector,
            rows,
            vector,
            rows,
            vector,
            vector,
            vector,
            rows,
            vector,
            rows,
            vector,
        ),
        check_vma=False,
    )
```

```python
from functools import partial
import math

import jax
import jax.numpy as jnp
from jax import lax
from jax.experimental import pallas as pl
from jax.experimental.pallas import tpu as pltpu
from jax.sharding import Mesh, PartitionSpec as P

HEADS = 16
HEAD = 64
EPSILON = 1e-05
SCALE = 1.0 / math.sqrt(HEAD)
AXES = ("y", "core", "z", "x")
NN = (((1,), (0,)), ((), ()))
NT = (((1,), (1,)), ((), ()))
TN = (((0,), (0,)), ((), ()))
LANES = 128
QUERIES = 128
REACH = 256
MASKED = -1e30
VMEM_LIMIT = 60 * 1024 * 1024
ANY = pl.BlockSpec(memory_space=pl.ANY)
SMEM = pl.BlockSpec(memory_space=pltpu.SMEM)


def dot(left, right, dims=NN):
    return lax.dot_general(left, right, dims, preferred_element_type=jnp.float32)


def params(limit=VMEM_LIMIT):
    return pltpu.CompilerParams(vmem_limit_bytes=limit)


def cost(flops, moved, special=0):
    return pl.CostEstimate(flops=int(flops), bytes_accessed=int(moved), transcendentals=int(special))


def ring(num):
    return [(place, (place + 1) % num) for place in range(num)]


class Grid:
    def __init__(self, sizes):
        self.sizes = dict(zip(AXES, sizes))
        self.total = math.prod(sizes)

    def coords(self):
        return {name: lax.axis_index(name) for name in AXES}

    def block(self, coords):
        place = 0
        for name in AXES:
            place = place * self.sizes[name] + coords[name]
        return place


def gather_pieces(grid, own, order):
    held = [own[None]]
    for name in order:
        held = [jnp.concatenate(held, 0) if len(held) > 1 else held[0]]
        for _ in range(grid.sizes[name] - 1):
            held.append(lax.ppermute(held[-1], name, ring(grid.sizes[name])))
    return held


def block_places(grid, coords, order):
    sizes = [grid.sizes[name] for name in order]
    places = []
    for slot in range(math.prod(sizes)):
        here = {}
        left = slot
        for name, size in zip(order, sizes):
            here[name] = lax.rem(coords[name] - left % size + size, size)
            left //= size
        places.append(grid.block(here))
    return jnp.stack(places).astype(jnp.int32)


class Gathered:
    def __init__(self, pieces, places):
        rows = pieces[0].shape[1]
        if rows % 16:
            blocks = jnp.concatenate(pieces, 0)
            placed = jnp.zeros_like(blocks).at[places].set(blocks)
            pieces = [placed.reshape(1, -1, blocks.shape[2])]
            places = jnp.zeros((1,), jnp.int32)
        self.pieces, self.places = list(pieces), places

    @property
    def count(self):
        return len(self.pieces)


def row_copies(places, pieces, first, target, column, width, sem):
    copies, number = [], 0
    for piece in pieces:
        blocks, rows, _ = piece.shape
        for slot in range(blocks):
            start = pl.multiple_of(places[number] * rows, rows)
            copies.append(
                pltpu.make_async_copy(
                    piece.at[slot, :, pl.ds(first, width)],
                    target.at[pl.ds(start, rows), pl.ds(column, width)],
                    sem,
                )
            )
            number += 1
    return copies


def scatter_stages(grid, coords, terms, axes, order, wire):
    axes = list(axes)
    for name in order:
        dim = axes.index(name)
        size = grid.sizes[name]
        arrived = None
        for step in range(size - 1):
            block = lax.rem(coords[name] + (2 * size - 1 - step), size)
            sent = sum(
                lax.dynamic_index_in_dim(term, block, dim, keepdims=False).astype(jnp.float32)
                for term in terms
            )
            if arrived is not None:
                sent = sent + arrived.astype(jnp.float32)
            arrived = lax.ppermute(sent.astype(wire), name, ring(size))
        terms = [
            lax.dynamic_index_in_dim(term, coords[name], dim, keepdims=False) for term in terms
        ] + [arrived]
        axes.remove(name)
    return sum(term.astype(jnp.float32) for term in terms)


def center_rows(rows):
    mean = jnp.mean(rows, axis=-1, keepdims=True)
    centred = rows - mean
    rate = lax.rsqrt(jnp.mean(centred * centred, axis=-1, keepdims=True) + EPSILON)
    return centred * rate, rate


def norm_pull(unit, rate, gain, cots):
    scaled = cots * gain
    return rate * (
        scaled
        - jnp.mean(scaled, axis=-1, keepdims=True)
        - unit * jnp.mean(scaled * unit, axis=-1, keepdims=True)
    )


def column_sum(values):
    return jnp.sum(values, axis=0, keepdims=True)


def gelu_parts(values):
    bell = jnp.exp(values * values * -0.5)
    t = 1.0 / (1.0 + jnp.abs(values) * (0.3275911 / math.sqrt(2.0)))
    series = t * (
        0.5 * 0.254829592
        + t
        * (
            0.5 * -0.284496736
            + t * (0.5 * 1.421413741 + t * (0.5 * -1.453152027 + t * (0.5 * 1.061405429)))
        )
    )
    tail = series * bell
    phi = jnp.where(values < 0.0, tail, 1.0 - tail)
    return values * phi, phi + values * bell * (1.0 / math.sqrt(2.0 * math.pi))


def project_kernel(counts, places_a, places_b, *refs):
    pieces_a, refs = refs[: counts[0]], refs[counts[0] :]
    pieces_b, refs = refs[: counts[1]], refs[counts[1] :]
    cells, gain, shift, bias, normed, qkv, weight, sem = refs
    width = cells.shape[1]
    copies = row_copies(places_a, pieces_a, 0, weight, 0, 2 * width, sem) + row_copies(
        places_b, pieces_b, 0, weight, 2 * width, width, sem
    )

    @pl.when(pl.program_id(0) == 0)
    def _():
        for copy in copies:
            copy.start()

    unit, _ = center_rows(cells[...].astype(jnp.float32))
    rows = (unit * gain[...] + shift[...]).astype(jnp.bfloat16)
    normed[...] = rows

    @pl.when(pl.program_id(0) == 0)
    def _():
        for copy in copies:
            copy.wait()

    for part in range(3):
        here = pl.ds(part * width, width)
        qkv[part] = (dot(rows, weight[:, here]) + bias[:, here]).astype(jnp.bfloat16)


def project(first, second, cells, gain, shift, bias, block=256):
    rows, width = cells.shape
    vector = pl.BlockSpec((1, width), lambda i: (0, 0))
    return pl.pallas_call(
        partial(project_kernel, (first.count, second.count)),
        grid=(rows // block,),
        in_specs=[SMEM, SMEM]
        + [ANY] * (first.count + second.count)
        + [
            pl.BlockSpec((block, width), lambda i: (i, 0)),
            vector,
            vector,
            pl.BlockSpec((1, 3 * width), lambda i: (0, 0)),
        ],
        out_specs=[
            pl.BlockSpec((block, width), lambda i: (i, 0)),
            pl.BlockSpec((3, block, width), lambda i: (0, i, 0)),
        ],
        out_shape=[
            jax.ShapeDtypeStruct((rows, width), jnp.bfloat16),
            jax.ShapeDtypeStruct((3, rows, width), jnp.bfloat16),
        ],
        scratch_shapes=[pltpu.VMEM((width, 3 * width), jnp.bfloat16), pltpu.SemaphoreType.DMA],
        compiler_params=params(),
        cost_estimate=cost(6 * rows * width * width, 10 * rows * width + 6 * width * width),
        name="project",
    )(
        first.places,
        second.places,
        *first.pieces,
        *second.pieces,
        cells,
        gain.reshape(1, -1),
        shift.reshape(1, -1),
        bias.reshape(1, -1),
    )


def key_range(first, rows):
    return max(0, first - REACH), min(rows, first + QUERIES + REACH)


def pair_rows(block, low):
    zero = jnp.zeros_like(block)
    return jnp.concatenate([jnp.where(low, block, zero), jnp.where(low, zero, block)], 0)


def twice(block, axis):
    return jnp.concatenate([block, block], axis)


def attend_kernel(ids_col, ids_row, live_row, qkv, mixed, log_sums, bias):
    rows = qkv.shape[1]

    @pl.when(pl.program_id(0) == 0)
    def _():
        for block, first in enumerate(range(0, rows, QUERIES)):
            start, stop = key_range(first, rows)
            shape = (QUERIES, stop - start)
            same = ids_col[first : first + QUERIES, :] == ids_row[:, start:stop]
            query_at = lax.broadcasted_iota(jnp.int32, shape, 0) + first
            key_at = lax.broadcasted_iota(jnp.int32, shape, 1) + start
            allowed = same & ((live_row[:, start:stop] == 1) | (query_at == key_at))
            bias[block, :, 0 : stop - start] = jnp.where(allowed, 0.0, MASKED)

    low = lax.broadcasted_iota(jnp.int32, (QUERIES, LANES), 1) < HEAD
    for block, first in enumerate(range(0, rows, QUERIES)):
        start, stop = key_range(first, rows)
        here = slice(first, first + QUERIES)
        query = pair_rows(qkv[0, here, :] * jnp.bfloat16(SCALE), low)
        scores = dot(query, qkv[1, start:stop, :], NT) + twice(bias[block, :, 0 : stop - start], 0)
        top = jnp.max(scores, axis=1, keepdims=True)
        expd = jnp.exp(scores - top)
        total = jnp.sum(expd, axis=1, keepdims=True)
        out = dot(expd.astype(jnp.bfloat16), qkv[2, start:stop, :]) / total
        mixed[here, :] = jnp.where(low, out[:QUERIES], out[QUERIES:]).astype(jnp.bfloat16)
        spread = jnp.broadcast_to(top + jnp.log(total), (2 * QUERIES, LANES)).T[0:1]
        log_sums[0, 0:1, here] = spread[:, :QUERIES]
        log_sums[0, 1:2, here] = spread[:, QUERIES:]


def attend(ids, live, qkv):
    _, rows, width = qkv.shape
    pairs = width // LANES
    whole = pl.BlockSpec((1, rows), lambda h: (0, 0))
    return pl.pallas_call(
        attend_kernel,
        grid=(pairs,),
        in_specs=[
            pl.BlockSpec((rows, 1), lambda h: (0, 0)),
            whole,
            whole,
            pl.BlockSpec((3, rows, LANES), lambda h: (0, 0, h)),
        ],
        out_specs=[
            pl.BlockSpec((rows, LANES), lambda h: (0, h)),
            pl.BlockSpec((1, 2, rows), lambda h: (h, 0, 0)),
        ],
        out_shape=[
            jax.ShapeDtypeStruct((rows, width), jnp.bfloat16),
            jax.ShapeDtypeStruct((pairs, 2, rows), jnp.float32),
        ],
        scratch_shapes=[
            pltpu.VMEM((rows // QUERIES, QUERIES, QUERIES + 2 * REACH), jnp.float32)
        ],
        compiler_params=params(),
        cost_estimate=cost(25 * 10**9, 8 * rows * width, 10**7),
        name="attend",
    )(ids.reshape(rows, 1), ids, live, qkv)


def attend_back_kernel(
    ids_col, ids_row, live_col, qkv, log_sums, d_mixed, d_qkv, sums, bias, d_key, d_value
):
    rows = qkv.shape[1]

    @pl.when(pl.program_id(0) == 0)
    def _():
        for block, first in enumerate(range(0, rows, QUERIES)):
            start, stop = key_range(first, rows)
            shape = (stop - start, QUERIES)
            same = ids_col[start:stop, :] == ids_row[:, first : first + QUERIES]
            query_at = lax.broadcasted_iota(jnp.int32, shape, 1) + first
            key_at = lax.broadcasted_iota(jnp.int32, shape, 0) + start
            allowed = same & ((live_col[start:stop, :] == 1) | (query_at == key_at))
            bias[block, 0 : stop - start, :] = jnp.where(allowed, 0.0, MASKED)

    d_key[...] = jnp.zeros_like(d_key)
    d_value[...] = jnp.zeros_like(d_value)
    low = lax.broadcasted_iota(jnp.int32, (QUERIES, LANES), 1) < HEAD
    query_sum = jnp.zeros((1, LANES), jnp.float32)
    for block, first in enumerate(range(0, rows, QUERIES)):
        start, stop = key_range(first, rows)
        here = slice(first, first + QUERIES)
        query = pair_rows(qkv[0, here, :] * jnp.bfloat16(SCALE), low)
        cot = pair_rows(d_mixed[here, :], low)
        keys, values = qkv[1, start:stop, :], qkv[2, start:stop, :]
        scores = dot(keys, query, NT) + twice(bias[block, 0 : stop - start, :], 1)
        ends = jnp.concatenate([log_sums[0, 0:1, here], log_sums[0, 1:2, here]], 1)
        probs = jnp.exp(scores - ends)
        weighted = probs * dot(values, cot, NT)
        d_scores = (weighted - probs * column_sum(weighted)).astype(jnp.bfloat16)
        d_value[start:stop, :] += dot(probs.astype(jnp.bfloat16), cot)
        d_key[start:stop, :] += dot(d_scores, query)
        both = dot(d_scores, keys, TN)
        d_query = (jnp.where(low, both[:QUERIES], both[QUERIES:]) * SCALE).astype(jnp.bfloat16)
        d_qkv[0, here, :] = d_query
        query_sum = query_sum + column_sum(d_query.astype(jnp.float32))
    d_qkv[1] = d_key[...].astype(jnp.bfloat16)
    value_low = d_value[...].astype(jnp.bfloat16)
    d_qkv[2] = value_low
    sums[0:1, :] = query_sum
    sums[1:2, :] = column_sum(value_low.astype(jnp.float32))


def attend_back(ids, live, qkv, log_sums, d_mixed):
    _, rows, width = qkv.shape
    pairs = width // LANES
    column = pl.BlockSpec((rows, 1), lambda h: (0, 0))
    triple = pl.BlockSpec((3, rows, LANES), lambda h: (0, 0, h))
    return pl.pallas_call(
        attend_back_kernel,
        grid=(pairs,),
        in_specs=[
            column,
            pl.BlockSpec((1, rows), lambda h: (0, 0)),
            column,
            triple,
            pl.BlockSpec((1, 2, rows), lambda h: (h, 0, 0)),
            pl.BlockSpec((rows, LANES), lambda h: (0, h)),
        ],
        out_specs=[triple, pl.BlockSpec((2, LANES), lambda h: (0, h))],
        out_shape=[
            jax.ShapeDtypeStruct(qkv.shape, jnp.bfloat16),
            jax.ShapeDtypeStruct((2, width), jnp.float32),
        ],
        scratch_shapes=[
            pltpu.VMEM((rows // QUERIES, QUERIES + 2 * REACH, QUERIES), jnp.float32),
            pltpu.VMEM((rows, LANES), jnp.float32),
            pltpu.VMEM((rows, LANES), jnp.float32),
        ],
        compiler_params=params(),
        cost_estimate=cost(38 * 10**9, 16 * rows * width, 10**7),
        name="attend_back",
    )(ids.reshape(rows, 1), ids, live.reshape(rows, 1), qkv, log_sums, d_mixed)


def feed_kernel(counts, chunk, places_out, places_up, places_down, *refs):
    pieces_out, refs = refs[: counts[0]], refs[counts[0] :]
    pieces_up, refs = refs[: counts[1]], refs[counts[1] :]
    pieces_down, refs = refs[: counts[2]], refs[counts[2] :]
    mixed, cells, out_grad, vectors, up_bias, refs = *refs[:5], refs[5:]
    normed, hidden, d_up, out_cells, d_inner, e_rows, d_mixed, sums, up_sums, refs = (
        *refs[:9],
        refs[9:],
    )
    w_out, w_up, w_down, slopes, sem_out, sem_up, sem_down = refs
    width, wide = w_up.shape
    out_copies = row_copies(places_out, pieces_out, width, w_out, 0, width, sem_out)
    up_copies = row_copies(places_up, pieces_up, 0, w_up, 0, wide, sem_up)
    down_copies = row_copies(places_down, pieces_down, 0, w_down, 0, width, sem_down)
    opening = pl.program_id(0) == 0

    @pl.when(opening)
    def _():
        for copy in out_copies + up_copies + down_copies:
            copy.start()
        sums[...] = jnp.zeros_like(sums)
        up_sums[...] = jnp.zeros_like(up_sums)
        for copy in out_copies:
            copy.wait()

    gain, shift = vectors[0:1, :], vectors[1:2, :]
    inner = cells[...].astype(jnp.float32) + dot(mixed[...], w_out[...]) + vectors[2:3, :]
    unit, rate = center_rows(inner)
    rows = (unit * gain + shift).astype(jnp.bfloat16)
    normed[...] = rows

    @pl.when(opening)
    def _():
        for copy in up_copies:
            copy.wait()

    for first in range(0, wide, chunk):
        here = slice(first, first + chunk)
        value, slope = gelu_parts(dot(rows, w_up[:, here]) + up_bias[:, here])
        hidden[:, here] = value.astype(jnp.bfloat16)
        slopes[:, here] = slope

    @pl.when(opening)
    def _():
        for copy in down_copies:
            copy.wait()

    layer_out = inner + dot(hidden[...], w_down[...]) + vectors[3:4, :]
    out_cells[...] = layer_out.astype(jnp.bfloat16)
    cot = out_grad[...]
    for first in range(0, wide, chunk):
        here = slice(first, first + chunk)
        slope = (dot(cot, w_down[here, :], NT) * slopes[:, here]).astype(jnp.bfloat16)
        d_up[:, here] = slope
        up_sums[:, here] += column_sum(slope.astype(jnp.float32))
    d_two = dot(d_up[...], w_up[...], NT)
    cot_wide = cot.astype(jnp.float32)
    pulled = cot_wide + norm_pull(unit, rate, gain, d_two)
    d_inner[...] = pulled
    low = pulled.astype(jnp.bfloat16)
    e_rows[...] = low
    d_mixed[...] = dot(low, w_out[...], NT).astype(jnp.bfloat16)
    sums[0:1, :] += column_sum(d_two * unit)
    sums[1:2, :] += column_sum(d_two)
    sums[2:3, :] += column_sum(low.astype(jnp.float32))
    sums[3:4, :] += column_sum(cot_wide)


def feed(out_w, up_w, down_w, mixed, cells, out_grad, vectors, up_bias, block=256, chunk=512):
    rows, width = cells.shape
    wide = up_bias.shape[0]
    narrow = pl.BlockSpec((block, width), lambda i: (i, 0))
    broad = pl.BlockSpec((block, wide), lambda i: (i, 0))
    low, full = jnp.bfloat16, jnp.float32
    struct = jax.ShapeDtypeStruct
    return pl.pallas_call(
        partial(feed_kernel, (out_w.count, up_w.count, down_w.count), chunk),
        grid=(rows // block,),
        in_specs=[SMEM] * 3
        + [ANY] * (out_w.count + up_w.count + down_w.count)
        + [
            narrow,
            narrow,
            narrow,
            pl.BlockSpec((4, width), lambda i: (0, 0)),
            pl.BlockSpec((1, wide), lambda i: (0, 0)),
        ],
        out_specs=[
            narrow,
            broad,
            broad,
            narrow,
            narrow,
            narrow,
            narrow,
            pl.BlockSpec((4, width), lambda i: (0, 0)),
            pl.BlockSpec((1, wide), lambda i: (0, 0)),
        ],
        out_shape=[
            struct((rows, width), low),
            struct((rows, wide), low),
            struct((rows, wide), low),
            struct((rows, width), low),
            struct((rows, width), full),
            struct((rows, width), low),
            struct((rows, width), low),
            struct((4, width), full),
            struct((1, wide), full),
        ],
        scratch_shapes=[
            pltpu.VMEM((width, width), low),
            pltpu.VMEM((width, wide), low),
            pltpu.VMEM((wide, width), low),
            pltpu.VMEM((block, wide), full),
            pltpu.SemaphoreType.DMA,
            pltpu.SemaphoreType.DMA,
            pltpu.SemaphoreType.DMA,
        ],
        compiler_params=params(),
        cost_estimate=cost(
            rows * width * (8 * wide + 4 * width), rows * (4 * wide + 20 * width) + 18 * 2**20, 10**7
        ),
        name="feed",
    )(
        out_w.places,
        up_w.places,
        down_w.places,
        *out_w.pieces,
        *up_w.pieces,
        *down_w.pieces,
        mixed,
        cells,
        out_grad,
        vectors,
        up_bias.reshape(1, -1),
    )


def grad_kernel(_, left, right, out):
    cots = right[...].reshape(right.shape[-2:])
    out[0] = dot(left[...], cots, TN).astype(out.dtype)


def half_grad(core, left, right, columns, outer, block=256, chunk=512):
    rows, width = left.shape
    per_outer = width // (2 * outer)
    block = min(block, per_outer)
    steps = per_outer // block
    first, span = columns
    depth = right.shape[-1] // chunk
    if right.ndim == 3:
        right_spec = pl.BlockSpec(
            (1, rows, chunk),
            lambda n, y, m, c: ((first // chunk + n) // depth, 0, (first // chunk + n) % depth),
        )
    else:
        right_spec = pl.BlockSpec((rows, chunk), lambda n, y, m, c: (0, first // chunk + n))
    return pl.pallas_call(
        grad_kernel,
        grid_spec=pltpu.PrefetchScalarGridSpec(
            num_scalar_prefetch=1,
            grid=(span // chunk, outer, steps),
            in_specs=[
                pl.BlockSpec((rows, block), lambda n, y, m, c: (0, (y * 2 + c[0]) * steps + m)),
                right_spec,
            ],
            out_specs=pl.BlockSpec((1, block, chunk), lambda n, y, m, c: (y, m, n)),
        ),
        out_shape=jax.ShapeDtypeStruct((outer, per_outer, span), jnp.bfloat16),
        compiler_params=params(),
        cost_estimate=cost(rows * width * span, rows * (width + 2 * span) + width * span),
        name="half_grad",
    )(core.reshape(1), left, right)


def weight_grad(grid, coords, left, right, columns):
    outer = grid.sizes["y"]

    def part(core):
        product = half_grad(core, left, right, columns, outer)
        return product.reshape(outer, grid.sizes["z"], grid.sizes["x"], -1, columns[1])

    sent = part(1 - coords["core"])
    arrived = lax.ppermute(sent, "core", ring(2))
    return [part(coords["core"]), arrived]


def cells_kernel(counts, places_a, places_b, *refs):
    pieces_a, refs = refs[: counts[0]], refs[counts[0] :]
    pieces_b, refs = refs[: counts[1]], refs[counts[1] :]
    d_qkv, cells, d_inner, gain, cells_grad, sums, weight, sem = refs
    width = cells.shape[1]
    copies = row_copies(places_a, pieces_a, 0, weight, 0, 2 * width, sem) + row_copies(
        places_b, pieces_b, 0, weight, 2 * width, width, sem
    )
    opening = pl.program_id(0) == 0

    @pl.when(opening)
    def _():
        for copy in copies:
            copy.start()
        sums[...] = jnp.zeros_like(sums)

    unit, rate = center_rows(cells[...].astype(jnp.float32))

    @pl.when(opening)
    def _():
        for copy in copies:
            copy.wait()

    d_one = sum(
        dot(d_qkv[part], weight[:, pl.ds(part * width, width)], NT) for part in range(3)
    )
    cells_grad[...] = (d_inner[...] + norm_pull(unit, rate, gain[...], d_one)).astype(jnp.bfloat16)
    sums[0:1, :] += column_sum(d_one * unit)
    sums[1:2, :] += column_sum(d_one)


def cells_back(first, second, d_qkv, cells, d_inner, gain, block=256):
    rows, width = cells.shape
    narrow = pl.BlockSpec((block, width), lambda i: (i, 0))
    return pl.pallas_call(
        partial(cells_kernel, (first.count, second.count)),
        grid=(rows // block,),
        in_specs=[SMEM, SMEM]
        + [ANY] * (first.count + second.count)
        + [
            pl.BlockSpec((3, block, width), lambda i: (0, i, 0)),
            narrow,
            narrow,
            pl.BlockSpec((1, width), lambda i: (0, 0)),
        ],
        out_specs=[narrow, pl.BlockSpec((2, width), lambda i: (0, 0))],
        out_shape=[
            jax.ShapeDtypeStruct((rows, width), jnp.bfloat16),
            jax.ShapeDtypeStruct((2, width), jnp.float32),
        ],
        scratch_shapes=[pltpu.VMEM((width, 3 * width), jnp.bfloat16), pltpu.SemaphoreType.DMA],
        compiler_params=params(),
        cost_estimate=cost(6 * rows * width * width, 14 * rows * width + 6 * width * width),
        name="cells_back",
    )(
        first.places,
        second.places,
        *first.pieces,
        *second.pieces,
        d_qkv,
        cells,
        d_inner,
        gain.reshape(1, -1),
    )


def local(
    grid,
    cells,
    segment_ids,
    valid,
    norm1_gain,
    norm1_bias,
    qkv_weight,
    qv_bias,
    out_weight,
    out_bias,
    norm2_gain,
    norm2_bias,
    up_weight,
    up_bias,
    down_weight,
    down_bias,
    out_grad,
):
    width = cells.shape[1]
    wide = up_weight.shape[1]
    coords = grid.coords()
    own_rows = qkv_weight.shape[0]
    order_a = ("x", "z", "y", "core")
    order_b = ("y", "z", "x", "core")
    places_a = block_places(grid, coords, order_a)
    places_b = block_places(grid, coords, order_b)
    vectors = (
        norm1_gain,
        norm1_bias,
        qv_bias,
        out_bias,
        norm2_gain,
        norm2_bias,
        up_bias,
        down_bias,
    )
    packed = jnp.concatenate(vectors)
    packed_size = packed.shape[0]
    packed = jnp.pad(packed, (0, own_rows * LANES - packed_size)).reshape(own_rows, LANES)
    w_up = lax.all_gather(up_weight, AXES, axis=0, tiled=True)
    pieces_a = gather_pieces(grid, qkv_weight[:, : 2 * width], order_a)
    pieces_b = gather_pieces(
        grid, jnp.concatenate([qkv_weight[:, 2 * width :], out_weight, packed], 1), order_b
    )
    queries_keys = Gathered(pieces_a, places_a)
    values_out = Gathered(pieces_b, places_b)
    down_own, _ = lax.optimization_barrier((down_weight, pieces_b[-1]))
    down_all = Gathered(gather_pieces(grid, down_own, order_a), places_a)
    up_all = Gathered([w_up[None]], jnp.zeros((1,), jnp.int32))

    arrived = jnp.concatenate(pieces_b, 0)[:, :, 2 * width :].reshape(grid.total, -1)
    arrived = jnp.zeros_like(arrived).at[places_b].set(arrived)[:, :packed_size]
    spread, first = [], 0
    for vector in vectors:
        size = vector.shape[0]
        spread.append(arrived[:, first : first + size].reshape(-1).astype(jnp.float32))
        first += size
    gain_one, shift_one, b_qv, b_out, gain_two, shift_two, b_up, b_down = spread

    qkv_bias = jnp.concatenate([b_qv[:width], jnp.zeros_like(b_out), b_qv[width:]])
    normed, qkv = project(queries_keys, values_out, cells, gain_one, shift_one, qkv_bias)
    mixed, log_sums = attend(segment_ids, valid, qkv)
    normed_two, hidden, d_up, out_cells, d_inner, e_rows, d_mixed, sums, up_sums = feed(
        values_out,
        up_all,
        down_all,
        mixed,
        cells,
        out_grad,
        jnp.stack([gain_two, shift_two, b_out, b_down]),
        b_up,
    )

    def total(terms, order):
        return scatter_stages(grid, coords, terms, ("y", "z", "x"), order, jnp.bfloat16)

    down_total = total(weight_grad(grid, coords, hidden, out_grad, (0, width)), ("x", "z", "y"))
    up_total = total(weight_grad(grid, coords, normed_two, d_up, (0, wide)), ("y", "z", "x"))
    out_total = total(weight_grad(grid, coords, mixed, e_rows, (0, width)), ("x", "z", "y"))
    d_qkv, qv_sums = attend_back(segment_ids, valid, qkv, log_sums, d_mixed)
    half = 3 * width // 2
    qkv_total = jnp.concatenate(
        [
            total(weight_grad(grid, coords, normed, d_qkv, (0, half)), ("x", "z", "y")),
            total(weight_grad(grid, coords, normed, d_qkv, (half, half)), ("y", "z", "x")),
        ],
        1,
    )
    cells_grad, one_sums = cells_back(queries_keys, values_out, d_qkv, cells, d_inner, gain_one)

    vector_grads = (
        one_sums[0],
        one_sums[1],
        qv_sums,
        sums[2],
        sums[0],
        sums[1],
        up_sums,
        sums[3],
    )
    sizes = [grid.sizes[name] for name in AXES]
    stacked = jnp.concatenate([grad.reshape(*sizes, -1) for grad in vector_grads], -1)
    summed = scatter_stages(
        grid, coords, [stacked], AXES, ("core", "x", "z", "y"), jnp.float32
    )
    parts, first = [], 0
    for vector in vectors:
        parts.append(summed[first : first + vector.shape[0]])
        first += vector.shape[0]
    return (
        out_cells,
        cells_grad,
        parts[0],
        parts[1],
        qkv_total,
        parts[2],
        out_total,
        parts[3],
        parts[4],
        parts[5],
        up_total,
        parts[6],
        down_total,
        parts[7],
    )


def solution(mesh):
    outer, inner_size = mesh.devices.shape
    sizes = (outer // 2, 2, inner_size // 2, 2)
    fine = Mesh(mesh.devices.reshape(sizes), AXES)
    rows, vector = P(AXES, None), P(AXES)
    return jax.shard_map(
        partial(local, Grid(sizes)),
        mesh=fine,
        in_specs=(
            rows,
            rows,
            rows,
            vector,
            vector,
            rows,
            vector,
            rows,
            vector,
            vector,
            vector,
            rows,
            vector,
            rows,
            vector,
            rows,
        ),
        out_specs=(
            rows,
            rows,
            vector,
            vector,
            rows,
            vector,
            rows,
            vector,
            vector,
            vector,
            rows,
            vector,
            rows,
            vector,
        ),
        check_vma=False,
    )
```

```python
from functools import partial
import itertools
import math

import jax
import jax.numpy as jnp
from jax import lax
from jax.experimental import pallas as pl
from jax.experimental.pallas import tpu as pltpu
from jax.sharding import Mesh, PartitionSpec as P

HEADS = 16
HEAD = 64
EPSILON = 1e-05
SCALE = 1.0 / math.sqrt(HEAD)
AXES = ("y", "core", "zh", "zl", "x")
NN = (((1,), (0,)), ((), ()))
NT = (((1,), (1,)), ((), ()))
TN = (((0,), (0,)), ((), ()))
LANES = 128
QUERIES = 128
REACH = 256
MASKED = -1e30
VMEM_LIMIT = 60 * 1024 * 1024
ANY = pl.BlockSpec(memory_space=pl.ANY)
SMEM = pl.BlockSpec(memory_space=pltpu.SMEM)


def dot(left, right, dims=NN):
    return lax.dot_general(left, right, dims, preferred_element_type=jnp.float32)


def params(limit=VMEM_LIMIT):
    return pltpu.CompilerParams(vmem_limit_bytes=limit)


def cost(flops, moved, special=0):
    return pl.CostEstimate(
        flops=int(flops) // 16, bytes_accessed=int(moved) // 16, transcendentals=int(special) // 16
    )


class Grid:
    def __init__(self, sizes):
        self.sizes = dict(zip(AXES, sizes))
        self.total = math.prod(sizes)

    def coords(self):
        return {name: lax.axis_index(name) for name in AXES}

    def block(self, coords):
        place = 0
        for name in AXES:
            place = place * self.sizes[name] + coords[name]
        return place


    def offsets(self, names):
        spans = [range(self.sizes[name]) for name in names]
        return [dict(zip(names, steps)) for steps in itertools.product(*spans) if any(steps)]

    def send(self, value, step):
        names = tuple(step)
        sizes = [self.sizes[name] for name in names]
        pairs = []
        for place in itertools.product(*[range(size) for size in sizes]):
            target = [(at + step[name]) % size for at, name, size in zip(place, names, sizes)]
            pairs.append((flat(place, sizes), flat(target, sizes)))
        return lax.ppermute(value, names, pairs)


def flat(place, sizes):
    index = 0
    for at, size in zip(place, sizes):
        index = index * size + at
    return index


def behind(grid, coords, step):
    return grid.block(
        {
            name: lax.rem(coords[name] + grid.sizes[name] - step.get(name, 0), grid.sizes[name])
            for name in AXES
        }
    )


def gather_near(grid, own):
    return jnp.stack([own] + [grid.send(own, step) for step in grid.offsets(("zh", "zl"))])


def gather_far(grid, line):
    arrived = [line] + [grid.send(line, step) for step in grid.offsets(("y", "x"))]
    return arrived, [grid.send(piece, {"core": 1}) for piece in arrived]


def gather_places(grid, coords):
    lines = [{}] + grid.offsets(("y", "x"))
    steps = lines + [{**line, "core": 1} for line in lines]
    near = [{}] + grid.offsets(("zh", "zl"))
    return jnp.stack(
        [behind(grid, coords, {**step, **deep}) for step in steps for deep in near]
    ).astype(jnp.int32)


class Gathered:
    def __init__(self, pieces, places):
        rows = pieces[0].shape[1]
        if rows % 16:
            blocks = jnp.concatenate(pieces, 0)
            placed = jnp.zeros_like(blocks).at[places].set(blocks)
            pieces = [placed.reshape(1, -1, blocks.shape[2])]
            places = jnp.zeros((1,), jnp.int32)
        self.pieces, self.places = list(pieces), places

    @property
    def count(self):
        return len(self.pieces)


def row_copies(places, pieces, first, target, column, width, sem):
    copies, number = [], 0
    for piece in pieces:
        blocks, rows, _ = piece.shape
        for slot in range(blocks):
            start = pl.multiple_of(places[number] * rows, rows)
            copies.append(
                pltpu.make_async_copy(
                    piece.at[slot, :, pl.ds(first, width)],
                    target.at[pl.ds(start, rows), pl.ds(column, width)],
                    sem,
                )
            )
            number += 1
    return copies


def pick(term, axes, places):
    starts = [places.get(name, 0) for name in axes] + [0] * (term.ndim - len(axes))
    shape = [1 if name in places else size for name, size in zip(axes, term.shape)]
    block = lax.dynamic_slice(term, starts, shape + list(term.shape[len(axes) :]))
    return block.reshape(
        [size for name, size in zip(axes, term.shape) if name not in places]
        + list(term.shape[len(axes) :])
    )


def add_up(terms):
    return sum(term.astype(jnp.float32) for term in terms)


class Scatter:
    def __init__(self, grid, coords, terms, axes):
        self.grid, self.coords, self.terms, self.axes = grid, coords, list(terms), tuple(axes)

    def sends(self, names, wire=jnp.bfloat16):
        self.names = names
        self.steps = self.grid.offsets(names)
        self.sent = [
            add_up(
                pick(
                    term,
                    self.axes,
                    {
                        name: lax.rem(self.coords[name] + step[name], self.grid.sizes[name])
                        for name in names
                    },
                )
                for term in self.terms
            ).astype(wire)
            for step in self.steps
        ]
        return self.sent

    def move(self):
        arrived = [self.grid.send(value, step) for value, step in zip(self.sent, self.steps)]
        own = {name: self.coords[name] for name in self.names}
        self.terms = [pick(term, self.axes, own) for term in self.terms] + arrived
        self.axes = tuple(name for name in self.axes if name not in self.names)
        return arrived

    def hold(self, token):
        self.terms = list(lax.optimization_barrier((self.terms, token))[0])

    def blocks(self, wire=jnp.bfloat16):
        lead = [self.axes.index(name) for name in ("zh", "zl")]
        value = add_up(jnp.moveaxis(term, lead, (0, 1)) for term in self.terms).astype(wire)
        self.left = value.reshape(-1, *value.shape[2:])
        return self.left

    def along_z(self):
        rows = self.left.reshape(-1, self.left.shape[-1])
        own = lax.psum_scatter(rows, ("zh", "zl"), scatter_dimension=0, tiled=True)
        return own.astype(jnp.float32).reshape(self.left.shape[1:])

    def total(self):
        return add_up(self.terms)


def center_rows(rows):
    mean = jnp.mean(rows, axis=-1, keepdims=True)
    centred = rows - mean
    rate = lax.rsqrt(jnp.mean(centred * centred, axis=-1, keepdims=True) + EPSILON)
    return centred * rate, rate


def norm_pull(unit, rate, gain, cots):
    scaled = cots * gain
    return rate * (
        scaled
        - jnp.mean(scaled, axis=-1, keepdims=True)
        - unit * jnp.mean(scaled * unit, axis=-1, keepdims=True)
    )


def column_sum(values):
    return jnp.sum(values, axis=0, keepdims=True)


def gelu_parts(values):
    phi = 0.5 + 0.5 * lax.erf(values * (1.0 / math.sqrt(2.0)))
    bell = jnp.exp(values * values * -0.5) * (1.0 / math.sqrt(2.0 * math.pi))
    return values * phi, phi + values * bell


def project_kernel(count, places, *refs):
    pieces, refs = refs[:count], refs[count:]
    cells, gain, shift, bias, normed, qkv, weight, sem = refs
    width = cells.shape[1]
    copies = row_copies(places, pieces, 0, weight, 0, 3 * width, sem)

    @pl.when(pl.program_id(0) == 0)
    def _():
        for copy in copies:
            copy.start()

    unit, _ = center_rows(cells[...].astype(jnp.float32))
    rows = (unit * gain[...] + shift[...]).astype(jnp.bfloat16)
    normed[...] = rows

    @pl.when(pl.program_id(0) == 0)
    def _():
        for copy in copies:
            copy.wait()

    for part in range(3):
        here = pl.ds(part * width, width)
        qkv[part] = (dot(rows, weight[:, here]) + bias[:, here]).astype(jnp.bfloat16)


def project(qkv_all, cells, gain, shift, bias, block=256):
    rows, width = cells.shape
    vector = pl.BlockSpec((1, width), lambda i: (0, 0))
    return pl.pallas_call(
        partial(project_kernel, qkv_all.count),
        grid=(rows // block,),
        in_specs=[SMEM]
        + [ANY] * qkv_all.count
        + [
            pl.BlockSpec((block, width), lambda i: (i, 0)),
            vector,
            vector,
            pl.BlockSpec((1, 3 * width), lambda i: (0, 0)),
        ],
        out_specs=[
            pl.BlockSpec((block, width), lambda i: (i, 0)),
            pl.BlockSpec((3, block, width), lambda i: (0, i, 0)),
        ],
        out_shape=[
            jax.ShapeDtypeStruct((rows, width), jnp.bfloat16),
            jax.ShapeDtypeStruct((3, rows, width), jnp.bfloat16),
        ],
        scratch_shapes=[pltpu.VMEM((width, 3 * width), jnp.bfloat16), pltpu.SemaphoreType.DMA],
        compiler_params=params(),
        cost_estimate=cost(6 * rows * width * width, 10 * rows * width + 6 * width * width),
        name="project",
    )(
        qkv_all.places,
        *qkv_all.pieces,
        cells,
        gain.reshape(1, -1),
        shift.reshape(1, -1),
        bias.reshape(1, -1),
    )


def key_range(first, rows):
    return max(0, first - REACH), min(rows, first + QUERIES + REACH)


def pair_rows(block, low):
    zero = jnp.zeros_like(block)
    return jnp.concatenate([jnp.where(low, block, zero), jnp.where(low, zero, block)], 0)


def twice(block, axis):
    return jnp.concatenate([block, block], axis)


def attend_kernel(count, ids_col, ids_row, live_row, qkv, *refs):
    mixed, log_sums, bias = refs[count:]
    rows = qkv.shape[1]

    @pl.when(pl.program_id(0) == 0)
    def _():
        for block, first in enumerate(range(0, rows, QUERIES)):
            start, stop = key_range(first, rows)
            shape = (QUERIES, stop - start)
            same = ids_col[first : first + QUERIES, :] == ids_row[:, start:stop]
            query_at = lax.broadcasted_iota(jnp.int32, shape, 0) + first
            key_at = lax.broadcasted_iota(jnp.int32, shape, 1) + start
            allowed = same & ((live_row[:, start:stop] == 1) | (query_at == key_at))
            bias[block, :, 0 : stop - start] = jnp.where(allowed, 0.0, MASKED)

    low = lax.broadcasted_iota(jnp.int32, (QUERIES, LANES), 1) < HEAD
    for block, first in enumerate(range(0, rows, QUERIES)):
        start, stop = key_range(first, rows)
        here = slice(first, first + QUERIES)
        query = pair_rows(qkv[0, here, :] * jnp.bfloat16(SCALE), low)
        scores = dot(query, qkv[1, start:stop, :], NT) + twice(bias[block, :, 0 : stop - start], 0)
        top = jnp.max(scores, axis=1, keepdims=True)
        expd = jnp.exp(scores - top)
        total = jnp.sum(expd, axis=1, keepdims=True)
        out = dot(expd.astype(jnp.bfloat16), qkv[2, start:stop, :]) / total
        mixed[here, :] = jnp.where(low, out[:QUERIES], out[QUERIES:]).astype(jnp.bfloat16)
        spread = jnp.broadcast_to(top + jnp.log(total), (2 * QUERIES, LANES)).T[0:1]
        log_sums[0, 0:1, here] = spread[:, :QUERIES]
        log_sums[0, 1:2, here] = spread[:, QUERIES:]


def attend(ids, live, qkv, after=()):
    _, rows, width = qkv.shape
    pairs = width // LANES
    whole = pl.BlockSpec((1, rows), lambda h: (0, 0))
    return pl.pallas_call(
        partial(attend_kernel, len(after)),
        grid=(pairs,),
        in_specs=[
            pl.BlockSpec((rows, 1), lambda h: (0, 0)),
            whole,
            whole,
            pl.BlockSpec((3, rows, LANES), lambda h: (0, 0, h)),
        ]
        + [ANY] * len(after),
        out_specs=[
            pl.BlockSpec((rows, LANES), lambda h: (0, h)),
            pl.BlockSpec((1, 2, rows), lambda h: (h, 0, 0)),
        ],
        out_shape=[
            jax.ShapeDtypeStruct((rows, width), jnp.bfloat16),
            jax.ShapeDtypeStruct((pairs, 2, rows), jnp.float32),
        ],
        scratch_shapes=[
            pltpu.VMEM((rows // QUERIES, QUERIES, QUERIES + 2 * REACH), jnp.float32)
        ],
        compiler_params=params(),
        cost_estimate=cost(25 * 10**9, 8 * rows * width, 10**7),
        name="attend",
    )(ids.reshape(rows, 1), ids, live, qkv, *after)


def attend_back_kernel(
    outer, count, core, ids_col, ids_row, live_col, qkv, log_sums, d_mixed, *refs
):
    lefts, refs = refs[: 2 * outer], refs[2 * outer + count :]
    d_qkv, sums, sent, kept, bias, d_key, d_value, turned, cots, query_sum = refs
    pair = pl.program_id(0)
    rows = qkv.shape[1]

    @pl.when(pair == 0)
    def _():
        for place, left in enumerate(lefts):
            block = left.shape[1]
            turned[place * block : (place + 1) * block, :] = left[...].T
        for block, first in enumerate(range(0, rows, QUERIES)):
            start, stop = key_range(first, rows)
            shape = (stop - start, QUERIES)
            same = ids_col[start:stop, :] == ids_row[:, first : first + QUERIES]
            query_at = lax.broadcasted_iota(jnp.int32, shape, 1) + first
            key_at = lax.broadcasted_iota(jnp.int32, shape, 0) + start
            allowed = same & ((live_col[start:stop, :] == 1) | (query_at == key_at))
            bias[block, 0 : stop - start, :] = jnp.where(allowed, 0.0, MASKED)

    d_key[...] = jnp.zeros_like(d_key)
    d_value[...] = jnp.zeros_like(d_value)
    low = lax.broadcasted_iota(jnp.int32, (QUERIES, LANES), 1) < HEAD
    query_sum[...] = jnp.zeros_like(query_sum)

    @pl.when(pair >= 0)
    def _():
        for block, first in enumerate(range(0, rows, QUERIES)):
            start, stop = key_range(first, rows)
            here = slice(first, first + QUERIES)
            query = pair_rows(qkv[0, here, :] * jnp.bfloat16(SCALE), low)
            cot = pair_rows(d_mixed[here, :], low)
            keys, values = qkv[1, start:stop, :], qkv[2, start:stop, :]
            scores = dot(keys, query, NT) + twice(bias[block, 0 : stop - start, :], 1)
            ends = jnp.concatenate([log_sums[0, 0:1, here], log_sums[0, 1:2, here]], 1)
            probs = jnp.exp(scores - ends)
            weighted = probs * dot(values, cot, NT)
            d_scores = (weighted - probs * column_sum(weighted)).astype(jnp.bfloat16)
            d_value[start:stop, :] += dot(probs.astype(jnp.bfloat16), cot)
            d_key[start:stop, :] += dot(d_scores, query)
            both = dot(d_scores, keys, TN)
            d_query = (jnp.where(low, both[:QUERIES], both[QUERIES:]) * SCALE).astype(jnp.bfloat16)
            d_qkv[0, here, :] = d_query
            query_sum[...] += column_sum(d_query.astype(jnp.float32))

    d_qkv[1] = d_key[...].astype(jnp.bfloat16)
    value_low = d_value[...].astype(jnp.bfloat16)
    d_qkv[2] = value_low
    odd = lax.rem(pair, 2)
    width = 2 * LANES
    for part in range(3):
        side = pl.ds(pl.multiple_of(part * width + odd * LANES, LANES), LANES)
        cots[:, side] = d_qkv[part]

    @pl.when(odd == 1)
    def _():
        half = turned.shape[0] // 2
        for out, first in ((sent, 0), (kept, half)):

            for begin in range(0, half, 256):
                side = slice(first + begin, first + begin + 256)
                grads = dot(turned[side, :], cots[...]).astype(jnp.bfloat16)
                for part in range(3):
                    out[part, begin : begin + 256, :] = grads[:, part * width : (part + 1) * width]

    sums[0:1, :] = query_sum[...]
    sums[1:2, :] = column_sum(value_low.astype(jnp.float32))


def attend_back(core, outer, ids, live, qkv, log_sums, d_mixed, normed, after=()):
    _, rows, width = qkv.shape
    pairs = width // LANES
    per_outer = normed.shape[1] // (2 * outer)
    column = pl.BlockSpec((rows, 1), lambda h, c: (0, 0))
    triple = pl.BlockSpec((3, rows, LANES), lambda h, c: (0, 0, h))
    grads = pl.BlockSpec((3, outer * per_outer, 2 * LANES), lambda h, c: (0, 0, h // 2))
    low, full, struct = jnp.bfloat16, jnp.float32, jax.ShapeDtypeStruct
    lefts = [
        pl.BlockSpec((rows, per_outer), lambda h, c, y=y: (0, y * 2 + 1 - c[0]))
        for y in range(outer)
    ] + [
        pl.BlockSpec((rows, per_outer), lambda h, c, y=y: (0, y * 2 + c[0])) for y in range(outer)
    ]
    grad_struct = struct((3, outer * per_outer, width), low)
    return pl.pallas_call(
        partial(attend_back_kernel, outer, len(after)),
        grid_spec=pltpu.PrefetchScalarGridSpec(
            num_scalar_prefetch=1,
            grid=(pairs,),
            in_specs=[
                column,
                pl.BlockSpec((1, rows), lambda h, c: (0, 0)),
                column,
                triple,
                pl.BlockSpec((1, 2, rows), lambda h, c: (h, 0, 0)),
                pl.BlockSpec((rows, LANES), lambda h, c: (0, h)),
            ]
            + lefts
            + [ANY] * len(after),
            out_specs=[triple, pl.BlockSpec((2, LANES), lambda h, c: (0, h)), grads, grads],
            scratch_shapes=[
                pltpu.VMEM((rows // QUERIES, QUERIES + 2 * REACH, QUERIES), full),
                pltpu.VMEM((rows, LANES), full),
                pltpu.VMEM((rows, LANES), full),
                pltpu.VMEM((2 * outer * per_outer, rows), low),
                pltpu.VMEM((rows, 6 * LANES), low),
                pltpu.VMEM((1, LANES), full),
            ],
        ),
        out_shape=[struct(qkv.shape, low), struct((2, width), full), grad_struct, grad_struct],
        compiler_params=params(),
        cost_estimate=cost(44 * 10**9, 28 * rows * width, 10**7),
        name="attend_back",
    )(
        core.reshape(1),
        ids.reshape(rows, 1),
        ids,
        live.reshape(rows, 1),
        qkv,
        log_sums,
        d_mixed,
        *[normed] * (2 * outer),
        *after,
    )


def feed_up_kernel(counts, chunk, places, *refs):
    pieces, refs = refs[: counts[0]], refs[counts[0] + counts[1] :]
    mixed, cells, vectors, up_bias, inner, normed, hidden, slopes = refs[:8]
    w_out, w_up, sem_out, sem_up = refs[8:]
    width, wide = w_up.shape
    out_copies = row_copies(places, pieces, wide, w_out, 0, width, sem_out)
    up_copies = row_copies(places, pieces, 0, w_up, 0, wide, sem_up)
    opening = pl.program_id(0) == 0

    @pl.when(opening)
    def _():
        for copy in out_copies + up_copies:
            copy.start()
        for copy in out_copies:
            copy.wait()

    stream = cells[...].astype(jnp.float32) + dot(mixed[...], w_out[...]) + vectors[2:3, :]
    inner[...] = stream
    unit, _ = center_rows(stream)
    rows = (unit * vectors[0:1, :] + vectors[1:2, :]).astype(jnp.bfloat16)
    normed[...] = rows

    @pl.when(opening)
    def _():
        for copy in up_copies:
            copy.wait()

    for first in range(0, wide, chunk):
        here = slice(first, first + chunk)
        value, slope = gelu_parts(dot(rows, w_up[:, here]) + up_bias[:, here])
        hidden[:, here] = value.astype(jnp.bfloat16)
        slopes[:, here] = slope.astype(jnp.bfloat16)


def feed_up(up_out, mixed, cells, vectors, up_bias, after=(), block=256, chunk=512):
    rows, width = cells.shape
    wide = up_bias.shape[0]
    narrow = pl.BlockSpec((block, width), lambda i: (i, 0))
    broad = pl.BlockSpec((block, wide), lambda i: (i, 0))
    low, struct = jnp.bfloat16, jax.ShapeDtypeStruct
    return pl.pallas_call(
        partial(feed_up_kernel, (up_out.count, len(after)), chunk),
        grid=(rows // block,),
        in_specs=[SMEM]
        + [ANY] * (up_out.count + len(after))
        + [
            narrow,
            narrow,
            pl.BlockSpec((4, width), lambda i: (0, 0)),
            pl.BlockSpec((1, wide), lambda i: (0, 0)),
        ],
        out_specs=[narrow, narrow, broad, broad],
        out_shape=[
            struct((rows, width), jnp.float32),
            struct((rows, width), low),
            struct((rows, wide), low),
            struct((rows, wide), low),
        ],
        scratch_shapes=[
            pltpu.VMEM((width, width), low),
            pltpu.VMEM((width, wide), low),
            pltpu.SemaphoreType.DMA,
            pltpu.SemaphoreType.DMA,
        ],
        compiler_params=params(),
        cost_estimate=cost(2 * rows * width * (wide + width), 32 * 2**20, 10**7),
        name="feed_up",
    )(up_out.places, *up_out.pieces, *after, mixed, cells, vectors, up_bias.reshape(1, -1))


def feed_down_kernel(counts, chunk, places_up, places_down, *refs):
    pieces_up, refs = refs[: counts[0]], refs[counts[0] :]
    pieces_down, refs = refs[: counts[1]], refs[counts[1] + counts[2] :]
    inner, hidden, slopes, out_grad, vectors = refs[:5]
    d_up, out_cells, d_inner, e_rows, d_mixed, sums, up_sums = refs[5:12]
    w_out, w_up, w_down, sem_out, sem_up, sem_down = refs[12:]
    width, wide = w_up.shape
    out_copies = row_copies(places_up, pieces_up, wide, w_out, 0, width, sem_out)
    up_copies = row_copies(places_up, pieces_up, 0, w_up, 0, wide, sem_up)
    down_copies = row_copies(places_down, pieces_down, 0, w_down, 0, width, sem_down)
    opening = pl.program_id(0) == 0

    @pl.when(opening)
    def _():
        for copy in down_copies + up_copies + out_copies:
            copy.start()
        sums[...] = jnp.zeros_like(sums)
        up_sums[...] = jnp.zeros_like(up_sums)
        for copy in down_copies:
            copy.wait()

    stream = inner[...]
    layer_out = stream + dot(hidden[...], w_down[...]) + vectors[3:4, :]
    out_cells[...] = layer_out.astype(jnp.bfloat16)
    cot = out_grad[...]
    for first in range(0, wide, chunk):
        here = slice(first, first + chunk)
        back = dot(cot, w_down[here, :], NT) * slopes[:, here].astype(jnp.float32)
        slope = back.astype(jnp.bfloat16)
        d_up[:, here] = slope
        up_sums[:, here] += column_sum(slope.astype(jnp.float32))

    @pl.when(opening)
    def _():
        for copy in up_copies + out_copies:
            copy.wait()

    d_two = dot(d_up[...], w_up[...], NT)
    unit, rate = center_rows(stream)
    cot_wide = cot.astype(jnp.float32)
    pulled = cot_wide + norm_pull(unit, rate, vectors[0:1, :], d_two)
    d_inner[...] = pulled
    low = pulled.astype(jnp.bfloat16)
    e_rows[...] = low
    d_mixed[...] = dot(low, w_out[...], NT).astype(jnp.bfloat16)
    sums[0:1, :] += column_sum(d_two * unit)
    sums[1:2, :] += column_sum(d_two)
    sums[2:3, :] += column_sum(low.astype(jnp.float32))
    sums[3:4, :] += column_sum(cot_wide)


def feed_down(
    up_out, down, inner, hidden, slopes, out_grad, vectors, after=(), block=256, chunk=512
):
    rows, width = inner.shape
    wide = hidden.shape[1]
    narrow = pl.BlockSpec((block, width), lambda i: (i, 0))
    broad = pl.BlockSpec((block, wide), lambda i: (i, 0))
    low, full, struct = jnp.bfloat16, jnp.float32, jax.ShapeDtypeStruct
    return pl.pallas_call(
        partial(feed_down_kernel, (up_out.count, down.count, len(after)), chunk),
        grid=(rows // block,),
        in_specs=[SMEM, SMEM]
        + [ANY] * (up_out.count + down.count + len(after))
        + [narrow, broad, broad, narrow, pl.BlockSpec((4, width), lambda i: (0, 0))],
        out_specs=[
            broad,
            narrow,
            narrow,
            narrow,
            narrow,
            pl.BlockSpec((4, width), lambda i: (0, 0)),
            pl.BlockSpec((1, wide), lambda i: (0, 0)),
        ],
        out_shape=[
            struct((rows, wide), low),
            struct((rows, width), low),
            struct((rows, width), full),
            struct((rows, width), low),
            struct((rows, width), low),
            struct((4, width), full),
            struct((1, wide), full),
        ],
        scratch_shapes=[
            pltpu.VMEM((width, width), low),
            pltpu.VMEM((width, wide), low),
            pltpu.VMEM((wide, width), low),
            pltpu.SemaphoreType.DMA,
            pltpu.SemaphoreType.DMA,
            pltpu.SemaphoreType.DMA,
        ],
        compiler_params=params(),
        cost_estimate=cost(2 * rows * width * (3 * wide + width), 58 * 2**20, 0),
        name="feed_down",
    )(
        up_out.places,
        down.places,
        *up_out.pieces,
        *down.pieces,
        *after,
        inner,
        hidden,
        slopes,
        out_grad,
        vectors,
    )


def grad_kernel(outer, ends, core, *refs):
    lefts, refs = refs[: outer * len(ends)], refs[outer * len(ends) :]
    rights, out, turned = refs[: len(ends)], refs[-2], refs[-1]
    chunk_at = pl.program_id(1)
    begin = 0
    for pair, end in enumerate(ends):

        @pl.when(chunk_at == begin)
        def _(pair=pair):
            for y in range(outer):
                left = lefts[pair * outer + y][...]
                turned[y * left.shape[1] : (y + 1) * left.shape[1], :] = left.T

        @pl.when((chunk_at >= begin) & (chunk_at < end))
        def _(pair=pair):
            cots = rights[pair][...].reshape(rights[pair].shape[-2:])
            out[...] = dot(turned[...], cots).astype(out.dtype).reshape(out.shape)

        begin = end


def half_grad(core, outer, pairs, after=(), block=256, chunk=1024):
    rows, width = pairs[0][0].shape
    per_outer = width // (2 * outer)
    block = min(block, per_outer)
    steps = per_outer // block
    ends, lefts, left_specs, right_specs, begin = [], [], [], [], 0
    for left, right, first, span in pairs:
        count, depth = span // chunk, right.shape[-1] // chunk
        for y in range(outer):
            lefts.append(left)
            left_specs.append(
                pl.BlockSpec(
                    (rows, block), lambda m, n, c, y=y: (0, (y * 2 + c[0]) * steps + m)
                )
            )

        def pick(n, begin=begin, count=count, first=first):
            return first // chunk + jnp.clip(n - begin, 0, count - 1)

        if right.ndim == 3:
            right_specs.append(
                pl.BlockSpec(
                    (1, rows, chunk),
                    lambda m, n, c, pick=pick, depth=depth: (pick(n) // depth, 0, pick(n) % depth),
                )
            )
        else:
            right_specs.append(
                pl.BlockSpec((rows, chunk), lambda m, n, c, pick=pick: (0, pick(n)))
            )
        begin += count
        ends.append(begin)
    total = begin * chunk

    def body(core, *refs):
        grad_kernel(outer, ends, core, *refs[: -2 - len(after)], *refs[-2:])

    return pl.pallas_call(
        body,
        grid_spec=pltpu.PrefetchScalarGridSpec(
            num_scalar_prefetch=1,
            grid=(steps, begin),
            in_specs=left_specs + right_specs + [ANY] * len(after),
            out_specs=pl.BlockSpec((outer, block, chunk), lambda m, n, c: (0, m, n)),
            scratch_shapes=[pltpu.VMEM((outer * block, rows), jnp.bfloat16)],
        ),
        out_shape=jax.ShapeDtypeStruct((outer, per_outer, total), jnp.bfloat16),
        compiler_params=params(),
        cost_estimate=cost(rows * width * total, rows * (width + 2 * total) + width * total),
        name="half_grad",
    )(core.reshape(1), *lefts, *[pair[1] for pair in pairs], *after)


def cells_kernel(counts, places, *refs):
    pieces, refs = refs[: counts[0]], refs[counts[0] + counts[1] :]
    d_qkv, cells, d_inner, gain, cells_grad, sums, weight, sem = refs
    width = cells.shape[1]
    copies = row_copies(places, pieces, 0, weight, 0, 3 * width, sem)
    opening = pl.program_id(0) == 0

    @pl.when(opening)
    def _():
        for copy in copies:
            copy.start()
        sums[...] = jnp.zeros_like(sums)

    unit, rate = center_rows(cells[...].astype(jnp.float32))

    @pl.when(opening)
    def _():
        for copy in copies:
            copy.wait()

    d_one = sum(
        dot(d_qkv[part], weight[:, pl.ds(part * width, width)], NT) for part in range(3)
    )
    cells_grad[...] = (d_inner[...] + norm_pull(unit, rate, gain[...], d_one)).astype(jnp.bfloat16)
    sums[0:1, :] += column_sum(d_one * unit)
    sums[1:2, :] += column_sum(d_one)


def cells_back(qkv_all, d_qkv, cells, d_inner, gain, after=(), block=256):
    rows, width = cells.shape
    narrow = pl.BlockSpec((block, width), lambda i: (i, 0))
    return pl.pallas_call(
        partial(cells_kernel, (qkv_all.count, len(after))),
        grid=(rows // block,),
        in_specs=[SMEM]
        + [ANY] * (qkv_all.count + len(after))
        + [
            pl.BlockSpec((3, block, width), lambda i: (0, i, 0)),
            narrow,
            narrow,
            pl.BlockSpec((1, width), lambda i: (0, 0)),
        ],
        out_specs=[narrow, pl.BlockSpec((2, width), lambda i: (0, 0))],
        out_shape=[
            jax.ShapeDtypeStruct((rows, width), jnp.bfloat16),
            jax.ShapeDtypeStruct((2, width), jnp.float32),
        ],
        scratch_shapes=[pltpu.VMEM((width, 3 * width), jnp.bfloat16), pltpu.SemaphoreType.DMA],
        compiler_params=params(),
        cost_estimate=cost(6 * rows * width * width, 14 * rows * width + 6 * width * width),
        name="cells_back",
    )(
        qkv_all.places,
        *qkv_all.pieces,
        *after,
        d_qkv,
        cells,
        d_inner,
        gain.reshape(1, -1),
    )


def local(
    grid,
    cells,
    segment_ids,
    valid,
    norm1_gain,
    norm1_bias,
    qkv_weight,
    qv_bias,
    out_weight,
    out_bias,
    norm2_gain,
    norm2_bias,
    up_weight,
    up_bias,
    down_weight,
    down_bias,
    out_grad,
):
    width = cells.shape[1]
    wide = up_weight.shape[1]
    coords = grid.coords()
    own_rows = qkv_weight.shape[0]
    places = gather_places(grid, coords)
    vectors = (
        norm1_gain,
        norm1_bias,
        qv_bias,
        out_bias,
        norm2_gain,
        norm2_bias,
        up_bias,
        down_bias,
    )
    groups = -(-len(vectors) // own_rows)
    packed = jnp.stack([jnp.pad(vector, (0, LANES - vector.shape[0])) for vector in vectors])
    packed = jnp.pad(packed, ((0, groups * own_rows - len(vectors)), (0, 0)))
    packed = packed.reshape(own_rows, groups * LANES)

    joined = lax.all_gather(
        jnp.concatenate([up_weight, out_weight], 1), AXES, axis=0, tiled=True
    )
    up_out = Gathered([joined[None]], jnp.zeros((1,), jnp.int32))
    line = gather_near(grid, jnp.concatenate([qkv_weight, packed], 1))
    near, far = gather_far(grid, line)
    qkv_all = Gathered(near + far, places)
    down_all = lax.all_gather(down_weight, AXES, axis=0, tiled=True)
    down_all = Gathered([down_all[None]], jnp.zeros((1,), jnp.int32))

    arrived = jnp.concatenate([piece[:, :, 3 * width :] for piece in near + far], 0)
    arrived = arrived.reshape(grid.total, groups * own_rows, LANES)[:, : len(vectors)]
    arrived = jnp.zeros_like(arrived).at[places].set(arrived)
    spread = [
        arrived[:, at, : vector.shape[0]].reshape(-1).astype(jnp.float32)
        for at, vector in enumerate(vectors)
    ]
    gain_one, shift_one, b_qv, b_out, gain_two, shift_two, b_up, b_down = spread
    rows_two = jnp.stack([gain_two, shift_two, b_out, b_down])

    qkv_bias = jnp.concatenate([b_qv[:width], jnp.zeros_like(b_out), b_qv[width:]])
    normed, qkv = project(qkv_all, cells, gain_one, shift_one, qkv_bias)
    mixed, log_sums = attend(segment_ids, valid, qkv)
    inner, normed_two, hidden, slopes = feed_up(up_out, mixed, cells, rows_two, b_up)

    mine, other = coords["core"], 1 - coords["core"]
    outer = grid.sizes["y"]
    block_axes = ("y", "zh", "zl", "x")
    block_sizes = [grid.sizes[name] for name in block_axes]

    def shared(product):
        return product.reshape(block_sizes + [-1, product.shape[-1]])

    def start(pairs, after=()):
        sent = half_grad(other, outer, pairs, after)
        return sent, grid.send(sent, {"core": 1})

    def under_way(kept, arrived):
        return Scatter(grid, coords, [shared(kept), shared(arrived)], block_axes)

    plane, side, deep = ("y", "x"), ("zl",), ("zh",)
    down_pairs = [(hidden, out_grad, 0, width)]
    down_sent, down_core = start(down_pairs)
    down_kept = half_grad(mine, outer, down_pairs, [down_sent])
    down_sum = under_way(down_kept, down_core)
    d_up, out_cells, d_inner, e_rows, d_mixed, sums, up_sums = feed_down(
        up_out, down_all, inner, hidden, slopes, out_grad, rows_two, down_sum.sends(plane)
    )
    down_sum.move()
    down_sum.hold(sums)
    up_pairs = [(normed_two, d_up, 0, wide), (mixed, e_rows, 0, width)]
    up_sent, up_core = start(up_pairs, [down_sum.blocks()])
    down_total = down_sum.along_z()
    up_kept = half_grad(mine, outer, up_pairs, [up_sent])
    up_sum = under_way(up_kept, up_core)
    d_qkv, qv_sums, qkv_sent, qkv_kept = attend_back(
        mine,
        outer,
        segment_ids,
        valid,
        qkv,
        log_sums,
        d_mixed,
        normed,
        up_sum.sends(plane),
    )
    up_sum.move()
    up_sum.hold(qv_sums)
    qkv_core = grid.send(qkv_sent, {"core": 1})
    qkv_sum = Scatter(
        grid,
        coords,
        [term.reshape([3] + block_sizes + [-1, width]) for term in (qkv_kept, qkv_core)],
        ("part",) + block_axes,
    )
    cells_grad, one_sums = cells_back(
        qkv_all,
        d_qkv,
        cells,
        d_inner,
        gain_one,
        qkv_sum.sends(plane) + [up_sum.blocks()],
    )
    up_total = up_sum.along_z()
    ahead = qkv_sum.move()
    qkv_sum.hold(one_sums)
    qkv_sum.blocks()
    qkv_total = qkv_sum.along_z()

    vector_grads = (
        one_sums[0],
        one_sums[1],
        qv_sums,
        sums[2],
        sums[0],
        sums[1],
        up_sums,
        sums[3],
    )
    sizes = [grid.sizes[name] for name in AXES]
    stacked = jnp.concatenate([grad.reshape(*sizes, -1) for grad in vector_grads], -1)
    stacked, _ = lax.optimization_barrier((stacked, ahead))
    vector_sum = Scatter(grid, coords, [stacked], AXES)
    for names in (("core",), plane, side, deep):
        vector_sum.sends(names, jnp.float32)
        vector_sum.move()
    summed = vector_sum.total()
    parts, first = [], 0
    for vector in vectors:
        parts.append(summed[first : first + vector.shape[0]])
        first += vector.shape[0]
    return (
        out_cells,
        cells_grad,
        parts[0],
        parts[1],
        jnp.concatenate([qkv_total[part] for part in range(3)], 1),
        parts[2],
        up_total[:, wide:],
        parts[3],
        parts[4],
        parts[5],
        up_total[:, :wide],
        parts[6],
        down_total,
        parts[7],
    )


def solution(mesh):
    outer, inner_size = mesh.devices.shape
    sizes = (outer // 2, 2, inner_size // 4, 2, 2)
    fine = Mesh(mesh.devices.reshape(sizes), AXES)
    rows, vector = P(AXES, None), P(AXES)
    return jax.shard_map(
        partial(local, Grid(sizes)),
        mesh=fine,
        in_specs=(
            rows,
            rows,
            rows,
            vector,
            vector,
            rows,
            vector,
            rows,
            vector,
            vector,
            vector,
            rows,
            vector,
            rows,
            vector,
            rows,
        ),
        out_specs=(
            rows,
            rows,
            vector,
            vector,
            rows,
            vector,
            rows,
            vector,
            vector,
            vector,
            rows,
            vector,
            rows,
            vector,
        ),
        check_vma=False,
    )
```

```python
from functools import partial
import itertools
import math

import jax
import jax.numpy as jnp
from jax import lax
from jax.experimental import pallas as pl
from jax.experimental.pallas import tpu as pltpu
from jax.sharding import Mesh, PartitionSpec as P

HEADS = 16
HEAD = 64
EPSILON = 1e-05
SCALE = 1.0 / math.sqrt(HEAD)
AXES = ("y", "core", "zh", "zl", "x")
NN = (((1,), (0,)), ((), ()))
NT = (((1,), (1,)), ((), ()))
TN = (((0,), (0,)), ((), ()))
LANES = 128
QUERIES = 128
REACH = 256
MASKED = -1e30
VMEM_LIMIT = 60 * 1024 * 1024
ANY = pl.BlockSpec(memory_space=pl.ANY)
SMEM = pl.BlockSpec(memory_space=pltpu.SMEM)


def dot(left, right, dims=NN):
    return lax.dot_general(left, right, dims, preferred_element_type=jnp.float32)


def params(limit=VMEM_LIMIT):
    return pltpu.CompilerParams(vmem_limit_bytes=limit)


def cost(flops, moved, special=0):
    return pl.CostEstimate(
        flops=int(flops) // 16, bytes_accessed=int(moved) // 16, transcendentals=int(special) // 16
    )


class Grid:
    def __init__(self, sizes):
        self.sizes = dict(zip(AXES, sizes))
        self.total = math.prod(sizes)

    def coords(self):
        return {name: lax.axis_index(name) for name in AXES}

    def block(self, coords):
        place = 0
        for name in AXES:
            place = place * self.sizes[name] + coords[name]
        return place


    def offsets(self, names):
        spans = [range(self.sizes[name]) for name in names]
        return [dict(zip(names, steps)) for steps in itertools.product(*spans) if any(steps)]

    def send(self, value, step):
        names = tuple(step)
        sizes = [self.sizes[name] for name in names]
        pairs = []
        for place in itertools.product(*[range(size) for size in sizes]):
            target = [(at + step[name]) % size for at, name, size in zip(place, names, sizes)]
            pairs.append((flat(place, sizes), flat(target, sizes)))
        return lax.ppermute(value, names, pairs)


def flat(place, sizes):
    index = 0
    for at, size in zip(place, sizes):
        index = index * size + at
    return index


def behind(grid, coords, step):
    return grid.block(
        {
            name: lax.rem(coords[name] + grid.sizes[name] - step.get(name, 0), grid.sizes[name])
            for name in AXES
        }
    )


hold = lax.optimization_barrier


def gather_near(grid, own, rounds=(("zh", "zl"),)):
    held = own[None]
    for names in rounds:
        arrived = [grid.send(held, step) for step in grid.offsets(names)]
        held = jnp.concatenate([held] + arrived, 0)
    return held


def gather_plane(grid, line):
    return [line] + [grid.send(line, step) for step in grid.offsets(("y", "x"))]


def gather_core(grid, lines):
    return [grid.send(piece, {"core": 1}) for piece in lines]


def gather_places(grid, coords, rounds=(("zh", "zl"),)):
    lines = [{}] + grid.offsets(("y", "x"))
    steps = lines + [{**line, "core": 1} for line in lines]
    near = [{}]
    for names in rounds:
        near = [{**step, **deep} for deep in [{}] + grid.offsets(names) for step in near]
    return jnp.stack(
        [behind(grid, coords, {**step, **deep}) for step in steps for deep in near]
    ).astype(jnp.int32)


class Gathered:
    def __init__(self, groups):
        rows = groups[0][0][0].shape[1]
        if rows % 16:
            columns = []
            for pieces, places, _, _ in groups:
                blocks = jnp.concatenate(pieces, 0)
                placed = jnp.zeros_like(blocks).at[places].set(blocks)
                columns.append(placed.reshape(-1, blocks.shape[2]))
            groups = [whole_group(jnp.concatenate(columns, 1))]
        self.pieces = [piece for group in groups for piece in group[0]]
        self.places = jnp.concatenate([group[1] for group in groups])
        self.layout = [
            ([piece.shape for piece in pieces], begin, end) for pieces, _, begin, end in groups
        ]

    @property
    def count(self):
        return len(self.pieces)


def whole_group(array):
    return [array[None]], jnp.zeros((1,), jnp.int32), 0, array.shape[1]


def row_copies(layout, places, pieces, first, target, width, sem):
    copies, number, at = [], 0, 0
    for shapes, begin, end in layout:
        low, high = max(first, begin), min(first + width, end)
        for blocks, rows, _ in shapes:
            for slot in range(blocks):
                if low < high:
                    start = pl.multiple_of(places[number] * rows, rows)
                    copies.append(
                        pltpu.make_async_copy(
                            pieces[at].at[slot, :, pl.ds(low - begin, high - low)],
                            target.at[pl.ds(start, rows), pl.ds(low - first, high - low)],
                            sem,
                        )
                    )
                number += 1
            at += 1
    return copies


def add_up(terms):
    return sum(term.astype(jnp.float32) for term in terms)


class Term:
    def __init__(self, array, axes, places=()):
        self.array, self.axes, self.places = array, axes, dict(places)

    def at(self, places):
        return Term(self.array, self.axes, {**self.places, **places})

    def value(self):
        axes, chosen, tail = self.axes, self.places, list(self.array.shape[len(self.axes) :])
        starts = [chosen.get(name, 0) for name in axes] + [0] * len(tail)
        sizes = dict(zip(axes, self.array.shape))
        shape = [1 if name in chosen else sizes[name] for name in axes]
        block = lax.dynamic_slice(self.array, starts, shape + tail)
        return block.reshape([sizes[name] for name in axes if name not in chosen] + tail)


class Scatter:
    plane = ("y", "x")

    def __init__(self, grid, coords, arrays, axes):
        self.grid, self.coords = grid, coords
        self.terms = [Term(array, axes) for array in arrays]
        self.steps = grid.offsets(self.plane)

    def sends(self, wire=jnp.bfloat16):
        self.sent = []
        for step in self.steps:
            target = {
                name: lax.rem(self.coords[name] + step[name], self.grid.sizes[name])
                for name in self.plane
            }
            self.sent.append(add_up(term.at(target).value() for term in self.terms).astype(wire))
        return self.sent

    def move(self, token):
        arrived = [self.grid.send(value, step) for value, step in zip(self.sent, self.steps)]
        arrived = hold((arrived, token))[0]
        own = {name: self.coords[name] for name in self.plane}
        self.terms = [term.at(own) for term in self.terms]
        axes = tuple(axis for axis in self.terms[0].axes if axis not in own)
        self.terms += [Term(value, axes) for value in arrived]
        return arrived

    def blocks(self, wire=jnp.bfloat16):
        axes = [axis for axis in self.terms[0].axes if axis not in self.terms[0].places]
        lead = [axes.index(name) for name in ("zh", "zl")]
        value = add_up(jnp.moveaxis(term.value(), lead, (0, 1)) for term in self.terms)
        self.left = value.astype(wire).reshape(-1, *value.shape[2:])
        return self.left

    def along_z(self):
        rows = self.left.reshape(-1, self.left.shape[-1])
        own = lax.psum_scatter(rows, ("zh", "zl"), scatter_dimension=0, tiled=True)
        return own.astype(jnp.float32).reshape(self.left.shape[1:])


def scatter_small(grid, coords, array, rounds):
    terms = [Term(array, AXES)]
    for names in rounds:
        steps = grid.offsets(names)
        sent = [
            add_up(
                term.at(
                    {name: lax.rem(coords[name] + step[name], grid.sizes[name]) for name in names}
                ).value()
                for term in terms
            )
            for step in steps
        ]
        arrived = [grid.send(value, step) for value, step in zip(sent, steps)]
        terms = [term.at({name: coords[name] for name in names}) for term in terms]
        axes = tuple(axis for axis in AXES if axis not in terms[0].places)
        terms += [Term(value, axes) for value in arrived]
    return add_up(term.value() for term in terms)


def center_rows(rows):
    mean = jnp.mean(rows, axis=-1, keepdims=True)
    centred = rows - mean
    rate = lax.rsqrt(jnp.mean(centred * centred, axis=-1, keepdims=True) + EPSILON)
    return centred * rate, rate


def norm_pull(unit, rate, gain, cots):
    scaled = cots * gain
    return rate * (
        scaled
        - jnp.mean(scaled, axis=-1, keepdims=True)
        - unit * jnp.mean(scaled * unit, axis=-1, keepdims=True)
    )


def column_sum(values):
    return jnp.sum(values, axis=0, keepdims=True)


def gelu_parts(values):
    phi = 0.5 + 0.5 * lax.erf(values * (1.0 / math.sqrt(2.0)))
    bell = jnp.exp(values * values * -0.5) * (1.0 / math.sqrt(2.0 * math.pi))
    return values * phi, phi + values * bell


def key_range(first, rows):
    return max(0, first - REACH), min(rows, first + QUERIES + REACH)


def pair_rows(block, low):
    zero = jnp.zeros_like(block)
    return jnp.concatenate([jnp.where(low, block, zero), jnp.where(low, zero, block)], 0)


def twice(block, axis):
    return jnp.concatenate([block, block], axis)


def attend_kernel(layout, counts, places, *refs):
    pieces, refs = refs[: counts[0]], refs[counts[0] + counts[1] :]
    cells, gain, shift, shift_qkv, ids_col, ids_row, live_row, refs = *refs[:7], refs[7:]
    normed, qkv, mixed, log_sums, weight, bias, sem = refs
    rows, width = cells.shape
    span = qkv.shape[2]
    step = pl.program_id(0)
    copies = row_copies(layout, places, pieces, 0, weight, 3 * width, sem)

    @pl.when(step == 0)
    def _():
        for copy in copies:
            copy.start()

        @pl.loop(0, rows // 256)
        def _(part):
            here = pl.ds(pl.multiple_of(part * 256, 256), 256)
            unit, _ = center_rows(cells[here, :].astype(jnp.float32))
            normed[here, :] = (unit * gain[...] + shift[...]).astype(jnp.bfloat16)

        for block, first in enumerate(range(0, rows, QUERIES)):
            start, stop = key_range(first, rows)
            shape = (QUERIES, stop - start)
            same = ids_col[first : first + QUERIES, :] == ids_row[:, start:stop]
            query_at = lax.broadcasted_iota(jnp.int32, shape, 0) + first
            key_at = lax.broadcasted_iota(jnp.int32, shape, 1) + start
            allowed = same & ((live_row[:, start:stop] == 1) | (query_at == key_at))
            bias[block, :, 0 : stop - start] = jnp.where(allowed, 0.0, MASKED)
        for copy in copies:
            copy.wait()

    @pl.when(step >= 0)
    def _():
        for part in range(3):
            here = pl.ds(pl.multiple_of(part * width + step * span, span), span)
            product = dot(normed[...], weight[:, here]) + shift_qkv[:, here]
            qkv[part] = product.astype(jnp.bfloat16)

    low = lax.broadcasted_iota(jnp.int32, (QUERIES, LANES), 1) < HEAD
    for pair in range(span // LANES):
        lanes = slice(pair * LANES, (pair + 1) * LANES)
        for block, first in enumerate(range(0, rows, QUERIES)):
            start, stop = key_range(first, rows)
            here = slice(first, first + QUERIES)
            query = pair_rows(qkv[0, here, lanes] * jnp.bfloat16(SCALE), low)
            scores = dot(query, qkv[1, start:stop, lanes], NT)
            scores = scores + twice(bias[block, :, 0 : stop - start], 0)
            top = jnp.max(scores, axis=1, keepdims=True)
            expd = jnp.exp(scores - top)
            total = jnp.sum(expd, axis=1, keepdims=True)
            out = dot(expd.astype(jnp.bfloat16), qkv[2, start:stop, lanes]) / total
            mixed[here, lanes] = jnp.where(low, out[:QUERIES], out[QUERIES:]).astype(jnp.bfloat16)
            spread = jnp.broadcast_to(top + jnp.log(total), (2 * QUERIES, LANES)).T[0:1]
            log_sums[pair, 0:1, here] = spread[:, :QUERIES]
            log_sums[pair, 1:2, here] = spread[:, QUERIES:]


def attend(qkv_all, cells, gain, shift, shift_qkv, ids, live, after=(), pairs=2):
    rows, width = cells.shape
    span = pairs * LANES
    row = pl.BlockSpec((1, rows), lambda h: (0, 0))
    vector = pl.BlockSpec((1, width), lambda h: (0, 0))
    whole = pl.BlockSpec((rows, width), lambda h: (0, 0))
    low, full, struct = jnp.bfloat16, jnp.float32, jax.ShapeDtypeStruct
    return pl.pallas_call(
        partial(attend_kernel, qkv_all.layout, (qkv_all.count, len(after))),
        grid=(width // span,),
        in_specs=[SMEM]
        + [ANY] * (qkv_all.count + len(after))
        + [
            whole,
            vector,
            vector,
            pl.BlockSpec((1, 3 * width), lambda h: (0, 0)),
            pl.BlockSpec((rows, 1), lambda h: (0, 0)),
            row,
            row,
        ],
        out_specs=[
            whole,
            pl.BlockSpec((3, rows, span), lambda h: (0, 0, h)),
            pl.BlockSpec((rows, span), lambda h: (0, h)),
            pl.BlockSpec((pairs, 2, rows), lambda h: (h, 0, 0)),
        ],
        out_shape=[
            struct((rows, width), low),
            struct((3, rows, width), low),
            struct((rows, width), low),
            struct((width // LANES, 2, rows), full),
        ],
        scratch_shapes=[
            pltpu.VMEM((width, 3 * width), low),
            pltpu.VMEM((rows // QUERIES, QUERIES, QUERIES + 2 * REACH), full),
            pltpu.SemaphoreType.DMA,
        ],
        compiler_params=params(),
        cost_estimate=cost(30 * 10**9, 18 * rows * width, 10**7),
        name="attend",
    )(
        qkv_all.places,
        *qkv_all.pieces,
        *after,
        cells,
        gain.reshape(1, -1),
        shift.reshape(1, -1),
        shift_qkv.reshape(1, -1),
        ids.reshape(rows, 1),
        ids,
        live,
    )


def attend_back_kernel(
    outer, count, core, ids_col, ids_row, live_col, qkv, log_sums, d_mixed, *refs
):
    lefts, refs = refs[: 2 * outer], refs[2 * outer + count :]
    d_qkv, sums, sent, kept, bias, d_key, d_value, turned, cots, query_sum = refs
    pair = pl.program_id(0)
    rows = qkv.shape[1]

    @pl.when(pair == 0)
    def _():
        for place, left in enumerate(lefts):
            block = left.shape[1]
            turned[place * block : (place + 1) * block, :] = left[...].T
        for block, first in enumerate(range(0, rows, QUERIES)):
            start, stop = key_range(first, rows)
            shape = (stop - start, QUERIES)
            same = ids_col[start:stop, :] == ids_row[:, first : first + QUERIES]
            query_at = lax.broadcasted_iota(jnp.int32, shape, 1) + first
            key_at = lax.broadcasted_iota(jnp.int32, shape, 0) + start
            allowed = same & ((live_col[start:stop, :] == 1) | (query_at == key_at))
            bias[block, 0 : stop - start, :] = jnp.where(allowed, 0.0, MASKED)

    d_key[...] = jnp.zeros_like(d_key)
    d_value[...] = jnp.zeros_like(d_value)
    low = lax.broadcasted_iota(jnp.int32, (QUERIES, LANES), 1) < HEAD
    query_sum[...] = jnp.zeros_like(query_sum)

    @pl.when(pair >= 0)
    def _():
        for block, first in enumerate(range(0, rows, QUERIES)):
            start, stop = key_range(first, rows)
            here = slice(first, first + QUERIES)
            query = pair_rows(qkv[0, here, :] * jnp.bfloat16(SCALE), low)
            cot = pair_rows(d_mixed[here, :], low)
            keys, values = qkv[1, start:stop, :], qkv[2, start:stop, :]
            scores = dot(keys, query, NT) + twice(bias[block, 0 : stop - start, :], 1)
            ends = jnp.concatenate([log_sums[0, 0:1, here], log_sums[0, 1:2, here]], 1)
            probs = jnp.exp(scores - ends)
            weighted = probs * dot(values, cot, NT)
            d_scores = (weighted - probs * column_sum(weighted)).astype(jnp.bfloat16)
            d_value[start:stop, :] += dot(probs.astype(jnp.bfloat16), cot)
            d_key[start:stop, :] += dot(d_scores, query)
            both = dot(d_scores, keys, TN)
            d_query = (jnp.where(low, both[:QUERIES], both[QUERIES:]) * SCALE).astype(jnp.bfloat16)
            d_qkv[0, here, :] = d_query
            query_sum[...] += column_sum(d_query.astype(jnp.float32))

    d_qkv[1] = d_key[...].astype(jnp.bfloat16)
    value_low = d_value[...].astype(jnp.bfloat16)
    d_qkv[2] = value_low
    odd = lax.rem(pair, 2)
    width = 2 * LANES
    for part in range(3):
        side = pl.ds(pl.multiple_of(part * width + odd * LANES, LANES), LANES)
        cots[:, side] = d_qkv[part]

    @pl.when(odd == 1)
    def _():
        half = turned.shape[0] // 2
        for out, first in ((sent, 0), (kept, half)):

            for begin in range(0, half, 256):
                side = slice(first + begin, first + begin + 256)
                grads = dot(turned[side, :], cots[...]).astype(jnp.bfloat16)
                for part in range(3):
                    out[part, begin : begin + 256, :] = grads[:, part * width : (part + 1) * width]

    sums[0:1, :] = query_sum[...]
    sums[1:2, :] = column_sum(value_low.astype(jnp.float32))


def attend_back(core, outer, ids, live, qkv, log_sums, d_mixed, normed, after=()):
    _, rows, width = qkv.shape
    pairs = width // LANES
    per_outer = normed.shape[1] // (2 * outer)
    column = pl.BlockSpec((rows, 1), lambda h, c: (0, 0))
    triple = pl.BlockSpec((3, rows, LANES), lambda h, c: (0, 0, h))
    grads = pl.BlockSpec((3, outer * per_outer, 2 * LANES), lambda h, c: (0, 0, h // 2))
    low, full, struct = jnp.bfloat16, jnp.float32, jax.ShapeDtypeStruct
    lefts = [
        pl.BlockSpec((rows, per_outer), lambda h, c, y=y: (0, y * 2 + 1 - c[0]))
        for y in range(outer)
    ] + [
        pl.BlockSpec((rows, per_outer), lambda h, c, y=y: (0, y * 2 + c[0])) for y in range(outer)
    ]
    grad_struct = struct((3, outer * per_outer, width), low)
    return pl.pallas_call(
        partial(attend_back_kernel, outer, len(after)),
        grid_spec=pltpu.PrefetchScalarGridSpec(
            num_scalar_prefetch=1,
            grid=(pairs,),
            in_specs=[
                column,
                pl.BlockSpec((1, rows), lambda h, c: (0, 0)),
                column,
                triple,
                pl.BlockSpec((1, 2, rows), lambda h, c: (h, 0, 0)),
                pl.BlockSpec((rows, LANES), lambda h, c: (0, h)),
            ]
            + lefts
            + [ANY] * len(after),
            out_specs=[triple, pl.BlockSpec((2, LANES), lambda h, c: (0, h)), grads, grads],
            scratch_shapes=[
                pltpu.VMEM((rows // QUERIES, QUERIES + 2 * REACH, QUERIES), full),
                pltpu.VMEM((rows, LANES), full),
                pltpu.VMEM((rows, LANES), full),
                pltpu.VMEM((2 * outer * per_outer, rows), low),
                pltpu.VMEM((rows, 6 * LANES), low),
                pltpu.VMEM((1, LANES), full),
            ],
        ),
        out_shape=[struct(qkv.shape, low), struct((2, width), full), grad_struct, grad_struct],
        compiler_params=params(),
        cost_estimate=cost(44 * 10**9, 28 * rows * width, 10**7),
        name="attend_back",
    )(
        core.reshape(1),
        ids.reshape(rows, 1),
        ids,
        live.reshape(rows, 1),
        qkv,
        log_sums,
        d_mixed,
        *[normed] * (2 * outer),
        *after,
    )


def feed_up_kernel(layout, counts, chunk, places, *refs):
    pieces, refs = refs[: counts[0]], refs[counts[0] + counts[1] :]
    mixed, cells, vectors, up_bias, inner, normed, hidden, slopes = refs[:8]
    w_out, w_up, sem_out, sem_up = refs[8:]
    width, wide = w_up.shape
    out_copies = row_copies(layout, places, pieces, wide, w_out, width, sem_out)
    up_copies = row_copies(layout, places, pieces, 0, w_up, wide, sem_up)
    opening = pl.program_id(0) == 0

    @pl.when(opening)
    def _():
        for copy in out_copies + up_copies:
            copy.start()
        for copy in out_copies:
            copy.wait()

    stream = cells[...].astype(jnp.float32) + dot(mixed[...], w_out[...]) + vectors[2:3, :]
    inner[...] = stream
    unit, _ = center_rows(stream)
    rows = (unit * vectors[0:1, :] + vectors[1:2, :]).astype(jnp.bfloat16)
    normed[...] = rows

    @pl.when(opening)
    def _():
        for copy in up_copies:
            copy.wait()

    for first in range(0, wide, chunk):
        here = slice(first, first + chunk)
        value, slope = gelu_parts(dot(rows, w_up[:, here]) + up_bias[:, here])
        hidden[:, here] = value.astype(jnp.bfloat16)
        slopes[:, here] = slope.astype(jnp.bfloat16)


def feed_up(up_out, mixed, cells, vectors, up_bias, after=(), block=256, chunk=512):
    rows, width = cells.shape
    wide = up_bias.shape[0]
    narrow = pl.BlockSpec((block, width), lambda i: (i, 0))
    broad = pl.BlockSpec((block, wide), lambda i: (i, 0))
    low, struct = jnp.bfloat16, jax.ShapeDtypeStruct
    return pl.pallas_call(
        partial(feed_up_kernel, up_out.layout, (up_out.count, len(after)), chunk),
        grid=(rows // block,),
        in_specs=[SMEM]
        + [ANY] * (up_out.count + len(after))
        + [
            narrow,
            narrow,
            pl.BlockSpec((4, width), lambda i: (0, 0)),
            pl.BlockSpec((1, wide), lambda i: (0, 0)),
        ],
        out_specs=[narrow, narrow, broad, broad],
        out_shape=[
            struct((rows, width), jnp.float32),
            struct((rows, width), low),
            struct((rows, wide), low),
            struct((rows, wide), low),
        ],
        scratch_shapes=[
            pltpu.VMEM((width, width), low),
            pltpu.VMEM((width, wide), low),
            pltpu.SemaphoreType.DMA,
            pltpu.SemaphoreType.DMA,
        ],
        compiler_params=params(),
        cost_estimate=cost(2 * rows * width * (wide + width), 32 * 2**20, 10**7),
        name="feed_up",
    )(up_out.places, *up_out.pieces, *after, mixed, cells, vectors, up_bias.reshape(1, -1))


def feed_down_kernel(layouts, counts, chunk, places_up, places_down, *refs):
    pieces_up, refs = refs[: counts[0]], refs[counts[0] :]
    pieces_down, refs = refs[: counts[1]], refs[counts[1] + counts[2] :]
    inner, slopes, out_grad, vectors = refs[:4]
    d_up, d_inner, e_rows, d_mixed, sums, up_sums = refs[4:10]
    w_out, w_up, w_down, sem_out, sem_up, sem_down = refs[10:]
    width, wide = w_up.shape
    out_copies = row_copies(layouts[0], places_up, pieces_up, wide, w_out, width, sem_out)
    up_copies = row_copies(layouts[0], places_up, pieces_up, 0, w_up, wide, sem_up)
    down_copies = row_copies(layouts[1], places_down, pieces_down, 0, w_down, width, sem_down)
    opening = pl.program_id(0) == 0

    @pl.when(opening)
    def _():
        for copy in down_copies + up_copies + out_copies:
            copy.start()
        sums[...] = jnp.zeros_like(sums)
        up_sums[...] = jnp.zeros_like(up_sums)
        for copy in down_copies:
            copy.wait()

    cot = out_grad[...]
    for first in range(0, wide, chunk):
        here = slice(first, first + chunk)
        back = dot(cot, w_down[here, :], NT) * slopes[:, here].astype(jnp.float32)
        slope = back.astype(jnp.bfloat16)
        d_up[:, here] = slope
        up_sums[:, here] += column_sum(slope.astype(jnp.float32))

    @pl.when(opening)
    def _():
        for copy in up_copies + out_copies:
            copy.wait()

    d_two = dot(d_up[...], w_up[...], NT)
    unit, rate = center_rows(inner[...])
    cot_wide = cot.astype(jnp.float32)
    pulled = cot_wide + norm_pull(unit, rate, vectors[0:1, :], d_two)
    d_inner[...] = pulled
    low = pulled.astype(jnp.bfloat16)
    e_rows[...] = low
    d_mixed[...] = dot(low, w_out[...], NT).astype(jnp.bfloat16)
    sums[0:1, :] += column_sum(d_two * unit)
    sums[1:2, :] += column_sum(d_two)
    sums[2:3, :] += column_sum(low.astype(jnp.float32))
    sums[3:4, :] += column_sum(cot_wide)


def feed_down(up_out, down, inner, slopes, out_grad, vectors, after=(), block=256, chunk=512):
    rows, width = inner.shape
    wide = slopes.shape[1]
    narrow = pl.BlockSpec((block, width), lambda i: (i, 0))
    broad = pl.BlockSpec((block, wide), lambda i: (i, 0))
    low, full, struct = jnp.bfloat16, jnp.float32, jax.ShapeDtypeStruct
    return pl.pallas_call(
        partial(
            feed_down_kernel,
            (up_out.layout, down.layout),
            (up_out.count, down.count, len(after)),
            chunk,
        ),
        grid=(rows // block,),
        in_specs=[SMEM, SMEM]
        + [ANY] * (up_out.count + down.count + len(after))
        + [narrow, broad, narrow, pl.BlockSpec((4, width), lambda i: (0, 0))],
        out_specs=[
            broad,
            narrow,
            narrow,
            narrow,
            pl.BlockSpec((4, width), lambda i: (0, 0)),
            pl.BlockSpec((1, wide), lambda i: (0, 0)),
        ],
        out_shape=[
            struct((rows, wide), low),
            struct((rows, width), full),
            struct((rows, width), low),
            struct((rows, width), low),
            struct((4, width), full),
            struct((1, wide), full),
        ],
        scratch_shapes=[
            pltpu.VMEM((width, width), low),
            pltpu.VMEM((width, wide), low),
            pltpu.VMEM((wide, width), low),
            pltpu.SemaphoreType.DMA,
            pltpu.SemaphoreType.DMA,
            pltpu.SemaphoreType.DMA,
        ],
        compiler_params=params(),
        cost_estimate=cost(2 * rows * width * (2 * wide + width), 48 * 2**20, 0),
        name="feed_down",
    )(
        up_out.places,
        down.places,
        *up_out.pieces,
        *down.pieces,
        *after,
        inner,
        slopes,
        out_grad,
        vectors,
    )


def output_kernel(layout, counts, places, *refs):
    pieces, refs = refs[: counts[0]], refs[counts[0] + counts[1] :]
    inner, hidden, shift, out_cells, weight, sem = refs
    copies = row_copies(layout, places, pieces, 0, weight, weight.shape[1], sem)

    @pl.when(pl.program_id(0) == 0)
    def _():
        for copy in copies:
            copy.start()
        for copy in copies:
            copy.wait()

    layer_out = inner[...] + dot(hidden[...], weight[...]) + shift[...]
    out_cells[...] = layer_out.astype(jnp.bfloat16)


def output(down, inner, hidden, shift, after=(), block=256):
    rows, width = inner.shape
    wide = hidden.shape[1]
    narrow = pl.BlockSpec((block, width), lambda i: (i, 0))
    return pl.pallas_call(
        partial(output_kernel, down.layout, (down.count, len(after))),
        grid=(rows // block,),
        in_specs=[SMEM]
        + [ANY] * (down.count + len(after))
        + [
            narrow,
            pl.BlockSpec((block, wide), lambda i: (i, 0)),
            pl.BlockSpec((1, width), lambda i: (0, 0)),
        ],
        out_specs=narrow,
        out_shape=jax.ShapeDtypeStruct((rows, width), jnp.bfloat16),
        scratch_shapes=[pltpu.VMEM((wide, width), jnp.bfloat16), pltpu.SemaphoreType.DMA],
        compiler_params=params(),
        cost_estimate=cost(2 * rows * width * wide, 24 * 2**20, 0),
        name="output",
    )(down.places, *down.pieces, *after, inner, hidden, shift.reshape(1, -1))


def grad_kernel(outer, ends, core, *refs):
    lefts, refs = refs[: outer * len(ends)], refs[outer * len(ends) :]
    rights, out, mark, turned = refs[: len(ends)], refs[-3], refs[-2], refs[-1]
    mark[...] = jnp.zeros_like(mark)
    chunk_at = pl.program_id(1)
    begin = 0
    for pair, end in enumerate(ends):

        @pl.when(chunk_at == begin)
        def _(pair=pair):
            for y in range(outer):
                left = lefts[pair * outer + y][...]
                turned[y * left.shape[1] : (y + 1) * left.shape[1], :] = left.T

        @pl.when((chunk_at >= begin) & (chunk_at < end))
        def _(pair=pair):
            cots = rights[pair][...].reshape(rights[pair].shape[-2:])
            out[...] = dot(turned[...], cots).astype(out.dtype).reshape(out.shape)

        begin = end


def half_grad(core, outer, pairs, after=(), block=256, chunk=1024):
    rows, width = pairs[0][0].shape
    per_outer = width // (2 * outer)
    block = min(block, per_outer)
    steps = per_outer // block
    ends, lefts, left_specs, right_specs, begin = [], [], [], [], 0
    for left, right, first, span in pairs:
        count, depth = span // chunk, right.shape[-1] // chunk
        for y in range(outer):
            lefts.append(left)
            left_specs.append(
                pl.BlockSpec(
                    (rows, block), lambda m, n, c, y=y: (0, (y * 2 + c[0]) * steps + m)
                )
            )

        def pick(n, begin=begin, count=count, first=first):
            return first // chunk + jnp.clip(n - begin, 0, count - 1)

        if right.ndim == 3:
            right_specs.append(
                pl.BlockSpec(
                    (1, rows, chunk),
                    lambda m, n, c, pick=pick, depth=depth: (pick(n) // depth, 0, pick(n) % depth),
                )
            )
        else:
            right_specs.append(
                pl.BlockSpec((rows, chunk), lambda m, n, c, pick=pick: (0, pick(n)))
            )
        begin += count
        ends.append(begin)
    total = begin * chunk

    def body(core, *refs):
        grad_kernel(outer, ends, core, *refs[: -3 - len(after)], *refs[-3:])

    return pl.pallas_call(
        body,
        grid_spec=pltpu.PrefetchScalarGridSpec(
            num_scalar_prefetch=1,
            grid=(steps, begin),
            in_specs=left_specs + right_specs + [ANY] * len(after),
            out_specs=[
                pl.BlockSpec((outer, block, chunk), lambda m, n, c: (0, m, n)),
                pl.BlockSpec((8, LANES), lambda m, n, c: (0, 0)),
            ],
            scratch_shapes=[pltpu.VMEM((outer * block, rows), jnp.bfloat16)],
        ),
        out_shape=[
            jax.ShapeDtypeStruct((outer, per_outer, total), jnp.bfloat16),
            jax.ShapeDtypeStruct((8, LANES), jnp.float32),
        ],
        compiler_params=params(),
        cost_estimate=cost(rows * width * total, rows * (width + 2 * total) + width * total),
        name="half_grad",
    )(core.reshape(1), *lefts, *[pair[1] for pair in pairs], *after)


def cells_kernel(layout, counts, places, *refs):
    pieces, refs = refs[: counts[0]], refs[counts[0] + counts[1] :]
    d_qkv, cells, d_inner, gain, cells_grad, sums, weight, sem = refs
    width = cells.shape[1]
    copies = row_copies(layout, places, pieces, 0, weight, 3 * width, sem)
    opening = pl.program_id(0) == 0

    @pl.when(opening)
    def _():
        for copy in copies:
            copy.start()
        sums[...] = jnp.zeros_like(sums)

    unit, rate = center_rows(cells[...].astype(jnp.float32))

    @pl.when(opening)
    def _():
        for copy in copies:
            copy.wait()

    d_one = sum(
        dot(d_qkv[part], weight[:, pl.ds(part * width, width)], NT) for part in range(3)
    )
    cells_grad[...] = (d_inner[...] + norm_pull(unit, rate, gain[...], d_one)).astype(jnp.bfloat16)
    sums[0:1, :] += column_sum(d_one * unit)
    sums[1:2, :] += column_sum(d_one)


def cells_back(qkv_all, d_qkv, cells, d_inner, gain, after=(), block=256):
    rows, width = cells.shape
    narrow = pl.BlockSpec((block, width), lambda i: (i, 0))
    return pl.pallas_call(
        partial(cells_kernel, qkv_all.layout, (qkv_all.count, len(after))),
        grid=(rows // block,),
        in_specs=[SMEM]
        + [ANY] * (qkv_all.count + len(after))
        + [
            pl.BlockSpec((3, block, width), lambda i: (0, i, 0)),
            narrow,
            narrow,
            pl.BlockSpec((1, width), lambda i: (0, 0)),
        ],
        out_specs=[narrow, pl.BlockSpec((2, width), lambda i: (0, 0))],
        out_shape=[
            jax.ShapeDtypeStruct((rows, width), jnp.bfloat16),
            jax.ShapeDtypeStruct((2, width), jnp.float32),
        ],
        scratch_shapes=[pltpu.VMEM((width, 3 * width), jnp.bfloat16), pltpu.SemaphoreType.DMA],
        compiler_params=params(),
        cost_estimate=cost(6 * rows * width * width, 14 * rows * width + 6 * width * width),
        name="cells_back",
    )(
        qkv_all.places,
        *qkv_all.pieces,
        *after,
        d_qkv,
        cells,
        d_inner,
        gain.reshape(1, -1),
    )


def local(
    grid,
    cells,
    segment_ids,
    valid,
    norm1_gain,
    norm1_bias,
    qkv_weight,
    qv_bias,
    out_weight,
    out_bias,
    norm2_gain,
    norm2_bias,
    up_weight,
    up_bias,
    down_weight,
    down_bias,
    out_grad,
):
    width = cells.shape[1]
    wide = up_weight.shape[1]
    coords = grid.coords()
    own_rows = qkv_weight.shape[0]
    places = gather_places(grid, coords)
    vectors = (
        norm1_gain,
        norm1_bias,
        qv_bias,
        out_bias,
        norm2_gain,
        norm2_bias,
        up_bias,
        down_bias,
    )
    groups = -(-len(vectors) // own_rows)
    packed = jnp.stack([jnp.pad(vector, (0, LANES - vector.shape[0])) for vector in vectors])
    packed = jnp.pad(packed, ((0, groups * own_rows - len(vectors)), (0, 0)))
    packed = packed.reshape(own_rows, groups * LANES)

    joined = lax.all_gather(
        jnp.concatenate([up_weight, out_weight], 1), AXES, axis=0, tiled=True
    )
    up_out = Gathered([whole_group(joined)])
    line = gather_near(grid, jnp.concatenate([qkv_weight, packed], 1))
    near = gather_plane(grid, line)
    qkv_pieces = near + gather_core(grid, near)
    qkv_all = Gathered([(qkv_pieces, places, 0, line.shape[2])])
    down_own, _ = hold((down_weight, near))
    down_all = lax.all_gather(down_own, AXES, axis=0, tiled=True)
    down_all = Gathered([whole_group(down_all)])

    arrived = jnp.concatenate([piece[:, :, 3 * width :] for piece in qkv_pieces], 0)
    arrived = arrived.reshape(grid.total, groups * own_rows, LANES)[:, : len(vectors)]
    arrived = jnp.zeros_like(arrived).at[places].set(arrived)
    unpacked = [
        arrived[:, at, : vector.shape[0]].reshape(-1).astype(jnp.float32)
        for at, vector in enumerate(vectors)
    ]
    gain_one, shift_one, b_qv, b_out, gain_two, shift_two, b_up, b_down = unpacked
    rows_two = jnp.stack([gain_two, shift_two, b_out, b_down])

    qkv_bias = jnp.concatenate([b_qv[:width], jnp.zeros_like(b_out), b_qv[width:]])
    normed, qkv, mixed, log_sums = attend(
        qkv_all, cells, gain_one, shift_one, qkv_bias, segment_ids, valid
    )
    inner, normed_two, hidden, slopes = feed_up(up_out, mixed, cells, rows_two, b_up)

    mine, other = coords["core"], 1 - coords["core"]
    outer = grid.sizes["y"]
    block_axes = ("y", "zh", "zl", "x")
    block_sizes = [grid.sizes[name] for name in block_axes]

    def shared(product):
        return product.reshape(block_sizes + [-1, product.shape[-1]])

    def start(pairs, after=()):
        sent, mark = half_grad(other, outer, pairs, after)
        return mark, grid.send(sent, {"core": 1})

    def under_way(kept, arrived):
        return Scatter(grid, coords, [shared(kept), shared(arrived)], block_axes)

    down_pairs = [(hidden, out_grad, 0, width)]
    down_mark, down_core = start(down_pairs)
    down_kept, _ = half_grad(mine, outer, down_pairs, [down_mark])
    down_sum = under_way(down_kept, down_core)
    d_up, d_inner, e_rows, d_mixed, sums, up_sums = feed_down(
        up_out, down_all, inner, slopes, out_grad, rows_two, down_sum.sends()
    )
    up_pairs = [(normed_two, d_up, 0, wide), (mixed, e_rows, 0, width)]
    down_sum.move(sums)
    up_mark, up_core = start(up_pairs, [down_sum.blocks()])
    down_total = down_sum.along_z()
    up_kept, _ = half_grad(mine, outer, up_pairs, [up_mark])
    up_sum = under_way(up_kept, up_core)
    d_qkv, qv_sums, qkv_sent, qkv_kept = attend_back(
        mine,
        outer,
        segment_ids,
        valid,
        qkv,
        log_sums,
        d_mixed,
        normed,
        up_sum.sends() + [down_total],
    )
    qkv_core = grid.send(qkv_sent, {"core": 1})
    qkv_sum = Scatter(
        grid,
        coords,
        [term.reshape([3] + block_sizes + [-1, width]) for term in (qkv_kept, qkv_core)],
        ("part",) + block_axes,
    )
    qkv_sends = qkv_sum.sends()
    up_moved = up_sum.move((qv_sums, qkv_sends[-1][:, 0, 0, :8, :LANES]))
    cells_grad, one_sums = cells_back(
        qkv_all, d_qkv, cells, d_inner, gain_one, qkv_sends + up_moved
    )
    up_blocks = up_sum.blocks()
    up_total = up_sum.along_z()
    out_cells = output(down_all, inner, hidden, b_down, [one_sums, up_blocks])
    ahead = qkv_sum.move(out_cells)
    qkv_sum.blocks()
    qkv_total = qkv_sum.along_z()

    vector_grads = (
        one_sums[0],
        one_sums[1],
        qv_sums,
        sums[2],
        sums[0],
        sums[1],
        up_sums,
        sums[3],
    )
    sizes = [grid.sizes[name] for name in AXES]
    stacked = jnp.concatenate([grad.reshape(*sizes, -1) for grad in vector_grads], -1)
    summed = scatter_small(
        grid, coords, stacked, (("core",), ("y", "x"), ("zl",), ("zh",))
    )
    parts, first = [], 0
    for vector in vectors:
        parts.append(summed[first : first + vector.shape[0]])
        first += vector.shape[0]
    return (
        out_cells,
        cells_grad,
        parts[0],
        parts[1],
        jnp.concatenate([qkv_total[part] for part in range(3)], 1),
        parts[2],
        up_total[:, wide:],
        parts[3],
        parts[4],
        parts[5],
        up_total[:, :wide],
        parts[6],
        down_total,
        parts[7],
    )


def solution(mesh):
    outer, inner_size = mesh.devices.shape
    sizes = (outer // 2, 2, inner_size // 4, 2, 2)
    fine = Mesh(mesh.devices.reshape(sizes), AXES)
    rows, vector = P(AXES, None), P(AXES)
    return jax.shard_map(
        partial(local, Grid(sizes)),
        mesh=fine,
        in_specs=(
            rows,
            rows,
            rows,
            vector,
            vector,
            rows,
            vector,
            rows,
            vector,
            vector,
            vector,
            rows,
            vector,
            rows,
            vector,
            rows,
        ),
        out_specs=(
            rows,
            rows,
            vector,
            vector,
            rows,
            vector,
            rows,
            vector,
            vector,
            vector,
            rows,
            vector,
            rows,
            vector,
        ),
        check_vma=False,
    )
```

```python
from functools import partial
import itertools
import math

import jax
import jax.numpy as jnp
from jax import lax
from jax.experimental import pallas as pl
from jax.experimental.pallas import tpu as pltpu
from jax.sharding import Mesh, PartitionSpec as P

HEADS = 16
HEAD = 64
EPSILON = 1e-05
SCALE = 1.0 / math.sqrt(HEAD)
AXES = ("y", "core", "zh", "zl", "x")
NN = (((1,), (0,)), ((), ()))
NT = (((1,), (1,)), ((), ()))
TN = (((0,), (0,)), ((), ()))
LANES = 128
QUERIES = 128
REACH = 256
MASKED = -1e30
VMEM_LIMIT = 60 * 1024 * 1024
ANY = pl.BlockSpec(memory_space=pl.ANY)
SMEM = pl.BlockSpec(memory_space=pltpu.SMEM)


def dot(left, right, dims=NN):
    return lax.dot_general(left, right, dims, preferred_element_type=jnp.float32)


def params(limit=VMEM_LIMIT):
    return pltpu.CompilerParams(vmem_limit_bytes=limit)


def cost(flops, moved, special=0):
    return pl.CostEstimate(
        flops=int(flops) // 16, bytes_accessed=int(moved) // 16, transcendentals=int(special) // 16
    )


class Grid:
    def __init__(self, sizes):
        self.sizes = dict(zip(AXES, sizes))
        self.total = math.prod(sizes)

    def coords(self):
        return {name: lax.axis_index(name) for name in AXES}

    def block(self, coords):
        place = 0
        for name in AXES:
            place = place * self.sizes[name] + coords[name]
        return place


    def offsets(self, names):
        spans = [range(self.sizes[name]) for name in names]
        return [dict(zip(names, steps)) for steps in itertools.product(*spans) if any(steps)]

    def send(self, value, step):
        names = tuple(step)
        sizes = [self.sizes[name] for name in names]
        pairs = []
        for place in itertools.product(*[range(size) for size in sizes]):
            target = [(at + step[name]) % size for at, name, size in zip(place, names, sizes)]
            pairs.append((flat(place, sizes), flat(target, sizes)))
        return lax.ppermute(value, names, pairs)


def flat(place, sizes):
    index = 0
    for at, size in zip(place, sizes):
        index = index * size + at
    return index


def behind(grid, coords, step):
    return grid.block(
        {
            name: lax.rem(coords[name] + grid.sizes[name] - step.get(name, 0), grid.sizes[name])
            for name in AXES
        }
    )


hold = lax.optimization_barrier


def gather_near(grid, own, rounds=(("zh", "zl"),)):
    held = own[None]
    for names in rounds:
        arrived = [grid.send(held, step) for step in grid.offsets(names)]
        held = jnp.concatenate([held] + arrived, 0)
    return held


def gather_plane(grid, line):
    return [line] + [grid.send(line, step) for step in grid.offsets(("y", "x"))]


def gather_core(grid, lines):
    return [grid.send(piece, {"core": 1}) for piece in lines]


def gather_places(grid, coords, rounds=(("zh", "zl"),)):
    lines = [{}] + grid.offsets(("y", "x"))
    steps = lines + [{**line, "core": 1} for line in lines]
    near = [{}]
    for names in rounds:
        near = [{**step, **deep} for deep in [{}] + grid.offsets(names) for step in near]
    return jnp.stack(
        [behind(grid, coords, {**step, **deep}) for step in steps for deep in near]
    ).astype(jnp.int32)


class Gathered:
    def __init__(self, groups):
        rows = groups[0][0][0].shape[1]
        if rows % 16:
            columns = []
            for pieces, places, _, _ in groups:
                blocks = jnp.concatenate(pieces, 0)
                placed = jnp.zeros_like(blocks).at[places].set(blocks)
                columns.append(placed.reshape(-1, blocks.shape[2]))
            groups = [whole_group(jnp.concatenate(columns, 1))]
        self.pieces = [piece for group in groups for piece in group[0]]
        self.places = jnp.concatenate([group[1] for group in groups])
        self.layout = [
            ([piece.shape for piece in pieces], begin, end) for pieces, _, begin, end in groups
        ]

    @property
    def count(self):
        return len(self.pieces)


def whole_group(array):
    return [array[None]], jnp.zeros((1,), jnp.int32), 0, array.shape[1]


def row_copies(layout, places, pieces, first, target, width, sem):
    copies, number, at = [], 0, 0
    for shapes, begin, end in layout:
        low, high = max(first, begin), min(first + width, end)
        for blocks, rows, _ in shapes:
            for slot in range(blocks):
                if low < high:
                    start = pl.multiple_of(places[number] * rows, rows)
                    copies.append(
                        pltpu.make_async_copy(
                            pieces[at].at[slot, :, pl.ds(low - begin, high - low)],
                            target.at[pl.ds(start, rows), pl.ds(low - first, high - low)],
                            sem,
                        )
                    )
                number += 1
            at += 1
    return copies


def add_up(terms):
    return sum(term.astype(jnp.float32) for term in terms)


class Term:
    def __init__(self, array, axes, places=()):
        self.array, self.axes, self.places = array, axes, dict(places)

    def at(self, places):
        return Term(self.array, self.axes, {**self.places, **places})

    def value(self):
        axes, chosen, tail = self.axes, self.places, list(self.array.shape[len(self.axes) :])
        starts = [chosen.get(name, 0) for name in axes] + [0] * len(tail)
        sizes = dict(zip(axes, self.array.shape))
        shape = [1 if name in chosen else sizes[name] for name in axes]
        block = lax.dynamic_slice(self.array, starts, shape + tail)
        return block.reshape([sizes[name] for name in axes if name not in chosen] + tail)


class Scatter:
    def __init__(self, grid, coords, arrays, axes):
        self.grid, self.coords = grid, coords
        self.terms = [Term(array, axes) for array in arrays]

    def sends(self, names, wire=jnp.bfloat16):
        self.names, self.steps, self.sent = names, self.grid.offsets(names), []
        for step in self.steps:
            target = {
                name: lax.rem(self.coords[name] + step[name], self.grid.sizes[name])
                for name in names
            }
            self.sent.append(add_up(term.at(target).value() for term in self.terms).astype(wire))
        return self.sent

    def move(self, token):
        arrived = [self.grid.send(value, step) for value, step in zip(self.sent, self.steps)]
        arrived, token = hold((arrived, token))
        own = {name: self.coords[name] for name in self.names}
        self.terms = [term.at(own) for term in self.terms]
        axes = tuple(axis for axis in self.terms[0].axes if axis not in self.terms[0].places)
        self.terms += [Term(value, axes) for value in arrived]
        return token

    def total(self):
        return add_up(term.value() for term in self.terms)

    def rows_z(self, wire=jnp.bfloat16):
        axes = [axis for axis in self.terms[0].axes if axis not in self.terms[0].places]
        lead = [axes.index(name) for name in ("zh", "zl")]
        value = add_up(jnp.moveaxis(term.value(), lead, (0, 1)) for term in self.terms)
        self.left = value.astype(wire).reshape(-1, *value.shape[2:])
        self.axes = tuple(axis for axis in axes if axis not in ("zh", "zl"))
        return self.left

    def along_z(self, token=None):
        rows = self.left.reshape(-1, self.left.shape[-1])
        own = lax.psum_scatter(rows, ("zh", "zl"), scatter_dimension=0, tiled=True)
        if token is not None:
            own, token = hold((own, token))
        self.terms = [Term(own.reshape(self.left.shape[1:]), self.axes)]
        return token


def joined_sides(first, second, token):
    arrays, _ = hold(([first.terms[0].value(), second.terms[0].value()], token))
    sizes, rows = arrays[0].shape[:2], arrays[1].shape[2]
    arrays = [array.reshape(*sizes, rows, -1) for array in arrays]
    return Scatter(first.grid, first.coords, [jnp.concatenate(arrays, -1)], first.axes)


def scatter_small(grid, coords, array, rounds):
    terms = [Term(array, AXES)]
    for names in rounds:
        steps = grid.offsets(names)
        sent = [
            add_up(
                term.at(
                    {name: lax.rem(coords[name] + step[name], grid.sizes[name]) for name in names}
                ).value()
                for term in terms
            )
            for step in steps
        ]
        arrived = [grid.send(value, step) for value, step in zip(sent, steps)]
        terms = [term.at({name: coords[name] for name in names}) for term in terms]
        axes = tuple(axis for axis in AXES if axis not in terms[0].places)
        terms += [Term(value, axes) for value in arrived]
    return add_up(term.value() for term in terms)


def center_rows(rows):
    mean = jnp.mean(rows, axis=-1, keepdims=True)
    centred = rows - mean
    rate = lax.rsqrt(jnp.mean(centred * centred, axis=-1, keepdims=True) + EPSILON)
    return centred * rate, rate


def norm_pull(unit, rate, gain, cots):
    scaled = cots * gain
    return rate * (
        scaled
        - jnp.mean(scaled, axis=-1, keepdims=True)
        - unit * jnp.mean(scaled * unit, axis=-1, keepdims=True)
    )


def column_sum(values):
    return jnp.sum(values, axis=0, keepdims=True)


def gelu_parts(values):
    phi = 0.5 + 0.5 * lax.erf(values * (1.0 / math.sqrt(2.0)))
    bell = jnp.exp(values * values * -0.5) * (1.0 / math.sqrt(2.0 * math.pi))
    return values * phi, phi + values * bell


def key_range(first, rows):
    return max(0, first - REACH), min(rows, first + QUERIES + REACH)


def pair_rows(block, low):
    zero = jnp.zeros_like(block)
    return jnp.concatenate([jnp.where(low, block, zero), jnp.where(low, zero, block)], 0)


def twice(block, axis):
    return jnp.concatenate([block, block], axis)


def attend_kernel(layout, counts, places, *refs):
    pieces, refs = refs[: counts[0]], refs[counts[0] + counts[1] :]
    cells, gain, shift, shift_qkv, ids_col, ids_row, live_row, refs = *refs[:7], refs[7:]
    normed, qkv, mixed, log_sums, weight, bias, sem = refs
    rows, width = cells.shape
    span = qkv.shape[2]
    step = pl.program_id(0)
    copies = row_copies(layout, places, pieces, 0, weight, 3 * width, sem)

    @pl.when(step == 0)
    def _():
        for copy in copies:
            copy.start()

        @pl.loop(0, rows // 256)
        def _(part):
            here = pl.ds(pl.multiple_of(part * 256, 256), 256)
            unit, _ = center_rows(cells[here, :].astype(jnp.float32))
            normed[here, :] = (unit * gain[...] + shift[...]).astype(jnp.bfloat16)

        for block, first in enumerate(range(0, rows, QUERIES)):
            start, stop = key_range(first, rows)
            shape = (QUERIES, stop - start)
            same = ids_col[first : first + QUERIES, :] == ids_row[:, start:stop]
            query_at = lax.broadcasted_iota(jnp.int32, shape, 0) + first
            key_at = lax.broadcasted_iota(jnp.int32, shape, 1) + start
            allowed = same & ((live_row[:, start:stop] == 1) | (query_at == key_at))
            bias[block, :, 0 : stop - start] = jnp.where(allowed, 0.0, MASKED)
        for copy in copies:
            copy.wait()

    @pl.when(step >= 0)
    def _():
        for part in range(3):
            here = pl.ds(pl.multiple_of(part * width + step * span, span), span)
            product = dot(normed[...], weight[:, here]) + shift_qkv[:, here]
            qkv[part] = product.astype(jnp.bfloat16)

    low = lax.broadcasted_iota(jnp.int32, (QUERIES, LANES), 1) < HEAD
    for pair in range(span // LANES):
        lanes = slice(pair * LANES, (pair + 1) * LANES)
        for block, first in enumerate(range(0, rows, QUERIES)):
            start, stop = key_range(first, rows)
            here = slice(first, first + QUERIES)
            query = pair_rows(qkv[0, here, lanes] * jnp.bfloat16(SCALE), low)
            scores = dot(query, qkv[1, start:stop, lanes], NT)
            scores = scores + twice(bias[block, :, 0 : stop - start], 0)
            top = jnp.max(scores, axis=1, keepdims=True)
            expd = jnp.exp(scores - top)
            total = jnp.sum(expd, axis=1, keepdims=True)
            out = dot(expd.astype(jnp.bfloat16), qkv[2, start:stop, lanes]) / total
            mixed[here, lanes] = jnp.where(low, out[:QUERIES], out[QUERIES:]).astype(jnp.bfloat16)
            spread = jnp.broadcast_to(top + jnp.log(total), (2 * QUERIES, LANES)).T[0:1]
            log_sums[pair, 0:1, here] = spread[:, :QUERIES]
            log_sums[pair, 1:2, here] = spread[:, QUERIES:]


def attend(qkv_all, cells, gain, shift, shift_qkv, ids, live, after=(), pairs=2):
    rows, width = cells.shape
    span = pairs * LANES
    row = pl.BlockSpec((1, rows), lambda h: (0, 0))
    vector = pl.BlockSpec((1, width), lambda h: (0, 0))
    whole = pl.BlockSpec((rows, width), lambda h: (0, 0))
    low, full, struct = jnp.bfloat16, jnp.float32, jax.ShapeDtypeStruct
    return pl.pallas_call(
        partial(attend_kernel, qkv_all.layout, (qkv_all.count, len(after))),
        grid=(width // span,),
        in_specs=[SMEM]
        + [ANY] * (qkv_all.count + len(after))
        + [
            whole,
            vector,
            vector,
            pl.BlockSpec((1, 3 * width), lambda h: (0, 0)),
            pl.BlockSpec((rows, 1), lambda h: (0, 0)),
            row,
            row,
        ],
        out_specs=[
            whole,
            pl.BlockSpec((3, rows, span), lambda h: (0, 0, h)),
            pl.BlockSpec((rows, span), lambda h: (0, h)),
            pl.BlockSpec((pairs, 2, rows), lambda h: (h, 0, 0)),
        ],
        out_shape=[
            struct((rows, width), low),
            struct((3, rows, width), low),
            struct((rows, width), low),
            struct((width // LANES, 2, rows), full),
        ],
        scratch_shapes=[
            pltpu.VMEM((width, 3 * width), low),
            pltpu.VMEM((rows // QUERIES, QUERIES, QUERIES + 2 * REACH), full),
            pltpu.SemaphoreType.DMA,
        ],
        compiler_params=params(),
        cost_estimate=cost(30 * 10**9, 18 * rows * width, 10**7),
        name="attend",
    )(
        qkv_all.places,
        *qkv_all.pieces,
        *after,
        cells,
        gain.reshape(1, -1),
        shift.reshape(1, -1),
        shift_qkv.reshape(1, -1),
        ids.reshape(rows, 1),
        ids,
        live,
    )


def attend_back_kernel(
    outer, count, core, ids_col, ids_row, live_col, qkv, log_sums, d_mixed, *refs
):
    lefts, refs = refs[: 2 * outer], refs[2 * outer + count :]
    d_qkv, sums, sent, kept, bias, d_key, d_value, turned, cots, query_sum = refs
    pair = pl.program_id(0)
    rows = qkv.shape[1]

    @pl.when(pair == 0)
    def _():
        for place, left in enumerate(lefts):
            block = left.shape[1]
            turned[place * block : (place + 1) * block, :] = left[...].T
        for block, first in enumerate(range(0, rows, QUERIES)):
            start, stop = key_range(first, rows)
            shape = (stop - start, QUERIES)
            same = ids_col[start:stop, :] == ids_row[:, first : first + QUERIES]
            query_at = lax.broadcasted_iota(jnp.int32, shape, 1) + first
            key_at = lax.broadcasted_iota(jnp.int32, shape, 0) + start
            allowed = same & ((live_col[start:stop, :] == 1) | (query_at == key_at))
            bias[block, 0 : stop - start, :] = jnp.where(allowed, 0.0, MASKED)

    d_key[...] = jnp.zeros_like(d_key)
    d_value[...] = jnp.zeros_like(d_value)
    low = lax.broadcasted_iota(jnp.int32, (QUERIES, LANES), 1) < HEAD
    query_sum[...] = jnp.zeros_like(query_sum)

    @pl.when(pair >= 0)
    def _():
        for block, first in enumerate(range(0, rows, QUERIES)):
            start, stop = key_range(first, rows)
            here = slice(first, first + QUERIES)
            query = pair_rows(qkv[0, here, :] * jnp.bfloat16(SCALE), low)
            cot = pair_rows(d_mixed[here, :], low)
            keys, values = qkv[1, start:stop, :], qkv[2, start:stop, :]
            scores = dot(keys, query, NT) + twice(bias[block, 0 : stop - start, :], 1)
            ends = jnp.concatenate([log_sums[0, 0:1, here], log_sums[0, 1:2, here]], 1)
            probs = jnp.exp(scores - ends)
            weighted = probs * dot(values, cot, NT)
            d_scores = (weighted - probs * column_sum(weighted)).astype(jnp.bfloat16)
            d_value[start:stop, :] += dot(probs.astype(jnp.bfloat16), cot)
            d_key[start:stop, :] += dot(d_scores, query)
            both = dot(d_scores, keys, TN)
            d_query = (jnp.where(low, both[:QUERIES], both[QUERIES:]) * SCALE).astype(jnp.bfloat16)
            d_qkv[0, here, :] = d_query
            query_sum[...] += column_sum(d_query.astype(jnp.float32))

    d_qkv[1] = d_key[...].astype(jnp.bfloat16)
    value_low = d_value[...].astype(jnp.bfloat16)
    d_qkv[2] = value_low
    odd = lax.rem(pair, 2)
    width = 2 * LANES
    for part in range(3):
        side = pl.ds(pl.multiple_of(part * width + odd * LANES, LANES), LANES)
        cots[:, side] = d_qkv[part]

    @pl.when(odd == 1)
    def _():
        half = turned.shape[0] // 2
        for out, first in ((sent, 0), (kept, half)):

            for begin in range(0, half, 256):
                side = slice(first + begin, first + begin + 256)
                grads = dot(turned[side, :], cots[...]).astype(jnp.bfloat16)
                for part in range(3):
                    out[part, begin : begin + 256, :] = grads[:, part * width : (part + 1) * width]

    sums[0:1, :] = query_sum[...]
    sums[1:2, :] = column_sum(value_low.astype(jnp.float32))


def attend_back(core, outer, ids, live, qkv, log_sums, d_mixed, normed, after=()):
    _, rows, width = qkv.shape
    pairs = width // LANES
    per_outer = normed.shape[1] // (2 * outer)
    column = pl.BlockSpec((rows, 1), lambda h, c: (0, 0))
    triple = pl.BlockSpec((3, rows, LANES), lambda h, c: (0, 0, h))
    grads = pl.BlockSpec((3, outer * per_outer, 2 * LANES), lambda h, c: (0, 0, h // 2))
    low, full, struct = jnp.bfloat16, jnp.float32, jax.ShapeDtypeStruct
    lefts = [
        pl.BlockSpec((rows, per_outer), lambda h, c, y=y: (0, y * 2 + 1 - c[0]))
        for y in range(outer)
    ] + [
        pl.BlockSpec((rows, per_outer), lambda h, c, y=y: (0, y * 2 + c[0])) for y in range(outer)
    ]
    grad_struct = struct((3, outer * per_outer, width), low)
    return pl.pallas_call(
        partial(attend_back_kernel, outer, len(after)),
        grid_spec=pltpu.PrefetchScalarGridSpec(
            num_scalar_prefetch=1,
            grid=(pairs,),
            in_specs=[
                column,
                pl.BlockSpec((1, rows), lambda h, c: (0, 0)),
                column,
                triple,
                pl.BlockSpec((1, 2, rows), lambda h, c: (h, 0, 0)),
                pl.BlockSpec((rows, LANES), lambda h, c: (0, h)),
            ]
            + lefts
            + [ANY] * len(after),
            out_specs=[triple, pl.BlockSpec((2, LANES), lambda h, c: (0, h)), grads, grads],
            scratch_shapes=[
                pltpu.VMEM((rows // QUERIES, QUERIES + 2 * REACH, QUERIES), full),
                pltpu.VMEM((rows, LANES), full),
                pltpu.VMEM((rows, LANES), full),
                pltpu.VMEM((2 * outer * per_outer, rows), low),
                pltpu.VMEM((rows, 6 * LANES), low),
                pltpu.VMEM((1, LANES), full),
            ],
        ),
        out_shape=[struct(qkv.shape, low), struct((2, width), full), grad_struct, grad_struct],
        compiler_params=params(),
        cost_estimate=cost(44 * 10**9, 28 * rows * width, 10**7),
        name="attend_back",
    )(
        core.reshape(1),
        ids.reshape(rows, 1),
        ids,
        live.reshape(rows, 1),
        qkv,
        log_sums,
        d_mixed,
        *[normed] * (2 * outer),
        *after,
    )


def feed_up_kernel(layout, counts, chunk, places, *refs):
    pieces, refs = refs[: counts[0]], refs[counts[0] + counts[1] :]
    mixed, cells, vectors, up_bias, inner, normed, hidden, slopes = refs[:8]
    w_out, w_up, sem_out, sem_up = refs[8:]
    width, wide = w_up.shape
    out_copies = row_copies(layout, places, pieces, wide, w_out, width, sem_out)
    up_copies = row_copies(layout, places, pieces, 0, w_up, wide, sem_up)
    opening = pl.program_id(0) == 0

    @pl.when(opening)
    def _():
        for copy in out_copies + up_copies:
            copy.start()
        for copy in out_copies:
            copy.wait()

    stream = cells[...].astype(jnp.float32) + dot(mixed[...], w_out[...]) + vectors[2:3, :]
    inner[...] = stream
    unit, _ = center_rows(stream)
    rows = (unit * vectors[0:1, :] + vectors[1:2, :]).astype(jnp.bfloat16)
    normed[...] = rows

    @pl.when(opening)
    def _():
        for copy in up_copies:
            copy.wait()

    for first in range(0, wide, chunk):
        here = slice(first, first + chunk)
        value, slope = gelu_parts(dot(rows, w_up[:, here]) + up_bias[:, here])
        hidden[:, here] = value.astype(jnp.bfloat16)
        slopes[:, here] = slope.astype(jnp.bfloat16)


def feed_up(up_out, mixed, cells, vectors, up_bias, after=(), block=256, chunk=512):
    rows, width = cells.shape
    wide = up_bias.shape[0]
    narrow = pl.BlockSpec((block, width), lambda i: (i, 0))
    broad = pl.BlockSpec((block, wide), lambda i: (i, 0))
    low, struct = jnp.bfloat16, jax.ShapeDtypeStruct
    return pl.pallas_call(
        partial(feed_up_kernel, up_out.layout, (up_out.count, len(after)), chunk),
        grid=(rows // block,),
        in_specs=[SMEM]
        + [ANY] * (up_out.count + len(after))
        + [
            narrow,
            narrow,
            pl.BlockSpec((4, width), lambda i: (0, 0)),
            pl.BlockSpec((1, wide), lambda i: (0, 0)),
        ],
        out_specs=[narrow, narrow, broad, broad],
        out_shape=[
            struct((rows, width), jnp.float32),
            struct((rows, width), low),
            struct((rows, wide), low),
            struct((rows, wide), low),
        ],
        scratch_shapes=[
            pltpu.VMEM((width, width), low),
            pltpu.VMEM((width, wide), low),
            pltpu.SemaphoreType.DMA,
            pltpu.SemaphoreType.DMA,
        ],
        compiler_params=params(),
        cost_estimate=cost(2 * rows * width * (wide + width), 32 * 2**20, 10**7),
        name="feed_up",
    )(up_out.places, *up_out.pieces, *after, mixed, cells, vectors, up_bias.reshape(1, -1))


def feed_down_kernel(layouts, counts, chunk, places_up, places_down, *refs):
    pieces_up, refs = refs[: counts[0]], refs[counts[0] :]
    pieces_down, refs = refs[: counts[1]], refs[counts[1] + counts[2] :]
    inner, slopes, out_grad, vectors = refs[:4]
    d_up, d_inner, e_rows, d_mixed, sums, up_sums = refs[4:10]
    w_out, w_up, w_down, sem_out, sem_up, sem_down = refs[10:]
    width, wide = w_up.shape
    out_copies = row_copies(layouts[0], places_up, pieces_up, wide, w_out, width, sem_out)
    up_copies = row_copies(layouts[0], places_up, pieces_up, 0, w_up, wide, sem_up)
    down_copies = row_copies(layouts[1], places_down, pieces_down, 0, w_down, width, sem_down)
    opening = pl.program_id(0) == 0

    @pl.when(opening)
    def _():
        for copy in down_copies + up_copies + out_copies:
            copy.start()
        sums[...] = jnp.zeros_like(sums)
        up_sums[...] = jnp.zeros_like(up_sums)
        for copy in down_copies:
            copy.wait()

    cot = out_grad[...]
    for first in range(0, wide, chunk):
        here = slice(first, first + chunk)
        back = dot(cot, w_down[here, :], NT) * slopes[:, here].astype(jnp.float32)
        slope = back.astype(jnp.bfloat16)
        d_up[:, here] = slope
        up_sums[:, here] += column_sum(slope.astype(jnp.float32))

    @pl.when(opening)
    def _():
        for copy in up_copies + out_copies:
            copy.wait()

    d_two = dot(d_up[...], w_up[...], NT)
    unit, rate = center_rows(inner[...])
    cot_wide = cot.astype(jnp.float32)
    pulled = cot_wide + norm_pull(unit, rate, vectors[0:1, :], d_two)
    d_inner[...] = pulled
    low = pulled.astype(jnp.bfloat16)
    e_rows[...] = low
    d_mixed[...] = dot(low, w_out[...], NT).astype(jnp.bfloat16)
    sums[0:1, :] += column_sum(d_two * unit)
    sums[1:2, :] += column_sum(d_two)
    sums[2:3, :] += column_sum(low.astype(jnp.float32))
    sums[3:4, :] += column_sum(cot_wide)


def feed_down(up_out, down, inner, slopes, out_grad, vectors, after=(), block=256, chunk=512):
    rows, width = inner.shape
    wide = slopes.shape[1]
    narrow = pl.BlockSpec((block, width), lambda i: (i, 0))
    broad = pl.BlockSpec((block, wide), lambda i: (i, 0))
    low, full, struct = jnp.bfloat16, jnp.float32, jax.ShapeDtypeStruct
    return pl.pallas_call(
        partial(
            feed_down_kernel,
            (up_out.layout, down.layout),
            (up_out.count, down.count, len(after)),
            chunk,
        ),
        grid=(rows // block,),
        in_specs=[SMEM, SMEM]
        + [ANY] * (up_out.count + down.count + len(after))
        + [narrow, broad, narrow, pl.BlockSpec((4, width), lambda i: (0, 0))],
        out_specs=[
            broad,
            narrow,
            narrow,
            narrow,
            pl.BlockSpec((4, width), lambda i: (0, 0)),
            pl.BlockSpec((1, wide), lambda i: (0, 0)),
        ],
        out_shape=[
            struct((rows, wide), low),
            struct((rows, width), full),
            struct((rows, width), low),
            struct((rows, width), low),
            struct((4, width), full),
            struct((1, wide), full),
        ],
        scratch_shapes=[
            pltpu.VMEM((width, width), low),
            pltpu.VMEM((width, wide), low),
            pltpu.VMEM((wide, width), low),
            pltpu.SemaphoreType.DMA,
            pltpu.SemaphoreType.DMA,
            pltpu.SemaphoreType.DMA,
        ],
        compiler_params=params(),
        cost_estimate=cost(2 * rows * width * (2 * wide + width), 48 * 2**20, 0),
        name="feed_down",
    )(
        up_out.places,
        down.places,
        *up_out.pieces,
        *down.pieces,
        *after,
        inner,
        slopes,
        out_grad,
        vectors,
    )


def output_kernel(layout, counts, places, *refs):
    pieces, refs = refs[: counts[0]], refs[counts[0] + counts[1] :]
    inner, hidden, shift, out_cells, weight, sem = refs
    copies = row_copies(layout, places, pieces, 0, weight, weight.shape[1], sem)

    @pl.when(pl.program_id(0) == 0)
    def _():
        for copy in copies:
            copy.start()
        for copy in copies:
            copy.wait()

    layer_out = inner[...] + dot(hidden[...], weight[...]) + shift[...]
    out_cells[...] = layer_out.astype(jnp.bfloat16)


def output(down, inner, hidden, shift, after=(), block=256):
    rows, width = inner.shape
    wide = hidden.shape[1]
    narrow = pl.BlockSpec((block, width), lambda i: (i, 0))
    return pl.pallas_call(
        partial(output_kernel, down.layout, (down.count, len(after))),
        grid=(rows // block,),
        in_specs=[SMEM]
        + [ANY] * (down.count + len(after))
        + [
            narrow,
            pl.BlockSpec((block, wide), lambda i: (i, 0)),
            pl.BlockSpec((1, width), lambda i: (0, 0)),
        ],
        out_specs=narrow,
        out_shape=jax.ShapeDtypeStruct((rows, width), jnp.bfloat16),
        scratch_shapes=[pltpu.VMEM((wide, width), jnp.bfloat16), pltpu.SemaphoreType.DMA],
        compiler_params=params(),
        cost_estimate=cost(2 * rows * width * wide, 24 * 2**20, 0),
        name="output",
    )(down.places, *down.pieces, *after, inner, hidden, shift.reshape(1, -1))


def grad_kernel(outer, sides, plan, *refs):
    span = outer * sides
    lefts, refs = refs[: span * len(plan)], refs[span * len(plan) :]
    count = sum(len(cuts) for _, cuts in plan)
    rights, refs = refs[: len(plan)], refs[-2 - sides * count :]
    outs, mark, turned = refs[:-2], refs[-2], refs[-1]
    mark[...] = jnp.zeros_like(mark)
    chunk_at = pl.program_id(1)
    begin, first_out = 0, 0
    for pair, (chunks, cuts) in enumerate(plan):

        @pl.when(chunk_at == begin)
        def _(pair=pair):
            for at in range(span):
                left = lefts[pair * span + at][...]
                turned[at * left.shape[1] : (at + 1) * left.shape[1], :] = left.T

        @pl.when((chunk_at >= begin) & (chunk_at < begin + chunks))
        def _(pair=pair, cuts=cuts, first_out=first_out):
            cots = rights[pair][...]
            rows = turned.shape[0] // sides
            for side in range(sides):
                grads = dot(turned[side * rows : (side + 1) * rows, :], cots).astype(jnp.bfloat16)
                column = 0
                for number, _ in enumerate(cuts):
                    out = outs[side * count + first_out + number]
                    wide = out.shape[2]
                    out[...] = grads[:, column : column + wide].reshape(out.shape)
                    column += wide

        begin += chunks
        first_out += len(cuts)


def core_grads(cores, outer, pairs, after=(), block=256, chunk=1024):
    rows, width = pairs[0][0].shape
    sides = len(cores)
    per_outer = width // (2 * outer)
    block = min(block, per_outer)
    steps = per_outer // block
    low, struct = jnp.bfloat16, jax.ShapeDtypeStruct
    plan, lefts, left_specs, right_specs, out_specs, outs, begin = [], [], [], [], [], [], 0
    for left, right, cuts in pairs:
        count = sum(cuts) // chunk
        for side in range(sides):
            for y in range(outer):
                lefts.append(left)
                left_specs.append(
                    pl.BlockSpec(
                        (rows, block),
                        lambda m, n, c, y=y, side=side: (0, (y * 2 + c[side]) * steps + m),
                    )
                )

        def at(n, begin=begin, count=count):
            return jnp.clip(n - begin, 0, count - 1)

        right_specs.append(pl.BlockSpec((rows, chunk), lambda m, n, c, at=at: (0, at(n))))
        for cut in cuts:
            out_specs.append(
                pl.BlockSpec((outer, block, min(cut, chunk)), lambda m, n, c, at=at: (0, m, at(n)))
            )
            outs.append(struct((outer, per_outer, cut), low))
        plan.append((count, cuts))
        begin += count
    total = begin * chunk

    def body(_, *refs):
        grad_kernel(outer, sides, plan, *refs)

    return pl.pallas_call(
        body,
        grid_spec=pltpu.PrefetchScalarGridSpec(
            num_scalar_prefetch=1,
            grid=(steps, begin),
            in_specs=left_specs + right_specs + [ANY] * len(after),
            out_specs=out_specs * sides + [pl.BlockSpec((8, LANES), lambda m, n, c: (0, 0))],
            scratch_shapes=[pltpu.VMEM((sides * outer * block, rows), low)],
        ),
        out_shape=outs * sides + [struct((8, LANES), jnp.float32)],
        compiler_params=params(),
        cost_estimate=cost(
            sides * rows * width * total,
            rows * (sides * width + 2 * total) + sides * width * total,
        ),
        name="core_grads",
    )(jnp.stack(cores), *lefts, *[pair[1] for pair in pairs], *after)


def cells_kernel(layout, counts, places, *refs):
    pieces, refs = refs[: counts[0]], refs[counts[0] + counts[1] :]
    d_qkv, cells, d_inner, gain, cells_grad, sums, weight, sem = refs
    width = cells.shape[1]
    copies = row_copies(layout, places, pieces, 0, weight, 3 * width, sem)
    opening = pl.program_id(0) == 0

    @pl.when(opening)
    def _():
        for copy in copies:
            copy.start()
        sums[...] = jnp.zeros_like(sums)

    unit, rate = center_rows(cells[...].astype(jnp.float32))

    @pl.when(opening)
    def _():
        for copy in copies:
            copy.wait()

    d_one = sum(
        dot(d_qkv[part], weight[:, pl.ds(part * width, width)], NT) for part in range(3)
    )
    cells_grad[...] = (d_inner[...] + norm_pull(unit, rate, gain[...], d_one)).astype(jnp.bfloat16)
    sums[0:1, :] += column_sum(d_one * unit)
    sums[1:2, :] += column_sum(d_one)


def cells_back(qkv_all, d_qkv, cells, d_inner, gain, after=(), block=256):
    rows, width = cells.shape
    narrow = pl.BlockSpec((block, width), lambda i: (i, 0))
    return pl.pallas_call(
        partial(cells_kernel, qkv_all.layout, (qkv_all.count, len(after))),
        grid=(rows // block,),
        in_specs=[SMEM]
        + [ANY] * (qkv_all.count + len(after))
        + [
            pl.BlockSpec((3, block, width), lambda i: (0, i, 0)),
            narrow,
            narrow,
            pl.BlockSpec((1, width), lambda i: (0, 0)),
        ],
        out_specs=[narrow, pl.BlockSpec((2, width), lambda i: (0, 0))],
        out_shape=[
            jax.ShapeDtypeStruct((rows, width), jnp.bfloat16),
            jax.ShapeDtypeStruct((2, width), jnp.float32),
        ],
        scratch_shapes=[pltpu.VMEM((width, 3 * width), jnp.bfloat16), pltpu.SemaphoreType.DMA],
        compiler_params=params(),
        cost_estimate=cost(6 * rows * width * width, 14 * rows * width + 6 * width * width),
        name="cells_back",
    )(
        qkv_all.places,
        *qkv_all.pieces,
        *after,
        d_qkv,
        cells,
        d_inner,
        gain.reshape(1, -1),
    )


def local(
    grid,
    cells,
    segment_ids,
    valid,
    norm1_gain,
    norm1_bias,
    qkv_weight,
    qv_bias,
    out_weight,
    out_bias,
    norm2_gain,
    norm2_bias,
    up_weight,
    up_bias,
    down_weight,
    down_bias,
    out_grad,
):
    width = cells.shape[1]
    wide = up_weight.shape[1]
    coords = grid.coords()
    own_rows = qkv_weight.shape[0]
    places = gather_places(grid, coords)
    vectors = (
        norm1_gain,
        norm1_bias,
        qv_bias,
        out_bias,
        norm2_gain,
        norm2_bias,
        up_bias,
        down_bias,
    )
    groups = -(-len(vectors) // own_rows)
    packed = jnp.stack([jnp.pad(vector, (0, LANES - vector.shape[0])) for vector in vectors])
    packed = jnp.pad(packed, ((0, groups * own_rows - len(vectors)), (0, 0)))
    packed = packed.reshape(own_rows, groups * LANES)

    joined = lax.all_gather(
        jnp.concatenate([up_weight, out_weight], 1), AXES, axis=0, tiled=True
    )
    up_out = Gathered([whole_group(joined)])
    line = gather_near(grid, jnp.concatenate([qkv_weight, packed], 1))
    near = gather_plane(grid, line)
    qkv_pieces = near + gather_core(grid, near)
    qkv_all = Gathered([(qkv_pieces, places, 0, line.shape[2])])
    down_own, _ = hold((down_weight, near))
    down_all = lax.all_gather(down_own, AXES, axis=0, tiled=True)
    down_all = Gathered([whole_group(down_all)])

    arrived = jnp.concatenate([piece[:, :, 3 * width :] for piece in qkv_pieces], 0)
    arrived = arrived.reshape(grid.total, groups * own_rows, LANES)[:, : len(vectors)]
    arrived = jnp.zeros_like(arrived).at[places].set(arrived)
    unpacked = [
        arrived[:, at, : vector.shape[0]].reshape(-1).astype(jnp.float32)
        for at, vector in enumerate(vectors)
    ]
    gain_one, shift_one, b_qv, b_out, gain_two, shift_two, b_up, b_down = unpacked
    rows_two = jnp.stack([gain_two, shift_two, b_out, b_down])

    qkv_bias = jnp.concatenate([b_qv[:width], jnp.zeros_like(b_out), b_qv[width:]])
    normed, qkv, mixed, log_sums = attend(
        qkv_all, cells, gain_one, shift_one, qkv_bias, segment_ids, valid
    )
    inner, normed_two, hidden, slopes = feed_up(up_out, mixed, cells, rows_two, b_up)

    mine, other = coords["core"], 1 - coords["core"]
    outer = grid.sizes["y"]
    block_axes = ("y", "zh", "zl", "x")
    block_sizes = [grid.sizes[name] for name in block_axes]

    def shared(product):
        return product.reshape(block_sizes + [-1, product.shape[-1]])

    def under_way(kept, sent):
        arrived = grid.send(sent, {"core": 1})
        return Scatter(grid, coords, [shared(kept), shared(arrived)], block_axes)

    plane, line_z = ("y", "x"), ("zh", "zl")
    quarter = width // 4
    down_pairs = [(hidden, out_grad, (width - quarter, quarter))]
    sent, sent_side, mark = core_grads([other], outer, down_pairs)
    kept, kept_side, _ = core_grads([mine], outer, down_pairs, [mark])
    down_sum, down_side = under_way(kept, sent), under_way(kept_side, sent_side)
    d_up, d_inner, e_rows, d_mixed, sums, up_sums = feed_down(
        up_out,
        down_all,
        inner,
        slopes,
        out_grad,
        rows_two,
        down_sum.sends(plane) + [down_side.rows_z()],
    )
    sums = down_sum.move(down_side.along_z(sums))
    up_pairs = [(normed_two, d_up, (wide,)), (mixed, e_rows, (width,))]
    sent, sent_side, kept, kept_side, _ = core_grads(
        [other, mine], outer, up_pairs, down_sum.sends(line_z)
    )
    sent, sent_side = down_sum.move((sent, sent_side))
    down_main = down_sum.total()
    up_sum, out_sum = under_way(kept, sent), under_way(kept_side, sent_side)
    d_qkv, qv_sums, qkv_sent, qkv_kept = attend_back(
        mine,
        outer,
        segment_ids,
        valid,
        qkv,
        log_sums,
        d_mixed,
        normed,
        up_sum.sends(plane) + [down_main, out_sum.rows_z(), down_side.terms[0].array],
    )
    qv_sums, qkv_sent = up_sum.move((qv_sums, qkv_sent))
    qkv_sent = out_sum.along_z(qkv_sent)
    qkv_core = grid.send(qkv_sent, {"core": 1})
    qkv_sum = Scatter(
        grid,
        coords,
        [term.reshape([3] + block_sizes + [-1, width]) for term in (qkv_kept, qkv_core)],
        ("part",) + block_axes,
    )
    cells_grad, one_sums = cells_back(
        qkv_all,
        d_qkv,
        cells,
        d_inner,
        gain_one,
        qkv_sum.sends(plane) + [up_sum.rows_z()],
    )
    vector_grads = (
        one_sums[0],
        one_sums[1],
        qv_sums,
        sums[2],
        sums[0],
        sums[1],
        up_sums,
        sums[3],
    )
    sizes = [grid.sizes[name] for name in AXES]
    stacked = jnp.concatenate([grad.reshape(*sizes, -1) for grad in vector_grads], -1)
    vector_sum = Scatter(grid, coords, [stacked], AXES)
    side_sum = joined_sides(down_side, out_sum, one_sums)
    out_cells = output(
        down_all,
        inner,
        hidden,
        b_down,
        vector_sum.sends(("core",), jnp.float32) + side_sum.sends(("y",)),
    )
    out_cells = qkv_sum.move(out_cells)
    qkv_sum.left = up_sum.along_z(side_sum.move(vector_sum.move(qkv_sum.rows_z())))
    up_total = up_sum.total()
    qkv_sum.along_z()
    vector_sum.sends(plane, jnp.float32)
    vector_sum.move(())
    vector_sum.sends(line_z, jnp.float32)
    vector_sum.move(())
    side_sum.sends(("x",))
    side_sum.move(())
    summed = vector_sum.total()
    qkv_total = qkv_sum.total()
    side_total = side_sum.total()
    rest = quarter * down_main.shape[0] // own_rows
    down_total = jnp.concatenate(
        [down_main, side_total[:, :rest].reshape(down_main.shape[0], quarter)], 1
    )
    out_total = side_total[:, rest:]
    parts, first = [], 0
    for vector in vectors:
        parts.append(summed[first : first + vector.shape[0]])
        first += vector.shape[0]
    return (
        out_cells,
        cells_grad,
        parts[0],
        parts[1],
        jnp.concatenate([qkv_total[part] for part in range(3)], 1),
        parts[2],
        out_total,
        parts[3],
        parts[4],
        parts[5],
        up_total,
        parts[6],
        down_total,
        parts[7],
    )


def solution(mesh):
    outer, inner_size = mesh.devices.shape
    sizes = (outer // 2, 2, inner_size // 4, 2, 2)
    fine = Mesh(mesh.devices.reshape(sizes), AXES)
    rows, vector = P(AXES, None), P(AXES)
    return jax.shard_map(
        partial(local, Grid(sizes)),
        mesh=fine,
        in_specs=(
            rows,
            rows,
            rows,
            vector,
            vector,
            rows,
            vector,
            rows,
            vector,
            vector,
            vector,
            rows,
            vector,
            rows,
            vector,
            rows,
        ),
        out_specs=(
            rows,
            rows,
            vector,
            vector,
            rows,
            vector,
            rows,
            vector,
            vector,
            vector,
            rows,
            vector,
            rows,
            vector,
        ),
        check_vma=False,
    )
```
